128 devices in a mesh: tm: 16 (over y, x_hi, core), unit: 8 (over x_lo, z).
Axes of the slice: x: 4 (x_hi: 2, x_lo: 2; x = x_hi * 2 + x_lo), y: 4, z: 4, core: 2. Of those that a mesh axis runs over, the one named last changes fastest.
Arguments:
- recording: bfloat16 [131072, 384], P(('tm', 'unit')), may hold values from -6 to 6
- spike_times: int32 [4096], P(('tm', 'unit')), may hold values from 30 to 131041, as said below
- unit_labels: int32 [4096], P(('tm', 'unit')), may hold values from 0 to 511, as said below
- old_templates: bfloat16 [512, 23424], P('unit'), may hold values from -3 to 3
Outputs:
- templates: bfloat16 [512, 23424], P('unit', 'tm')
- scores: float32 [512, 65536], P('unit', 'tm')
The draws below stay inside these ranges and needn't reach their ends.
Inputs may be any that keep to these rules, and one draw needn't show every extreme that they name: `spike_times`: the spikes lie in blocks of 32, block b on the device of flattened index b over tm and unit; the times of block b lie in b * 1024 + 30 to (b + 1) * 1024 - 31, and both ends are reached in every block. `unit_labels`: labels lie in 0 to 511; the panel of a label is label // 64. In each block of 32 spikes at most 8 labels fall in one panel, and on each index of tm one panel receives exactly 8 from every block of that index.
All inputs are finite; a program needn't handle non-finite values.
Results may differ from the reference program's by a relative error of at most 0.0027.
Values may be sent and summed in bfloat16 or wider, within the bound.
A program may use at most 64 MiB of HBM per device.

```python
import jax
import jax.numpy as jnp
from jax import lax

C = 384
TAPS = 61
PANEL = 64
STRIDE = 2
SPK_DEV = 32
CAP = 8
OWNERS = 8
UNITS = 512
FEAT = 23424
HALF = 30
SLAB = 8192
SAMPLES = 131072
WINDOWS = 65536
SPIKES = 4096


def draw_spike_times(key, part):
    blocks = SPIKES // SPK_DEV
    sub = SLAB // OWNERS

    def one_block(index):
        lower = index * sub + HALF
        upper = index * sub + sub - HALF
        values = jax.random.randint(jax.random.fold_in(key, index), (SPK_DEV,), lower, upper)
        places = jnp.arange(SPK_DEV)
        values = jnp.where(places == 0, upper - 1, values)
        values = jnp.where(places == 1, lower, values)
        return values
    return jax.vmap(one_block)(jnp.arange(blocks)).reshape(-1).astype(jnp.int32)


def draw_unit_labels(key, part):
    blocks = SPIKES // SPK_DEV
    hot_key = jax.random.fold_in(key, 7)
    base_key = jax.random.fold_in(key, 11)

    def one_block(index):
        row = index // OWNERS
        hot = jax.random.randint(jax.random.fold_in(hot_key, row), (), 0, OWNERS)
        block_key = jax.random.fold_in(base_key, index)
        first_key, second_key, third_key = jax.random.split(block_key, 3)
        others = jnp.arange((OWNERS - 1) * CAP) // CAP
        others = others + (others >= hot).astype(others.dtype)
        taken = jax.random.permutation(first_key, others)[:SPK_DEV - CAP]
        owner_list = jnp.concatenate([jnp.full((CAP,), hot, others.dtype), taken])
        owner_list = jax.random.permutation(second_key, owner_list)
        within = jax.random.randint(third_key, (SPK_DEV,), 0, PANEL)
        return owner_list * PANEL + within
    return jax.vmap(one_block)(jnp.arange(blocks)).reshape(-1).astype(jnp.int32)


def block_scale(rng, shape, pieces, low, largest):
    def one(position, shards_of):
        heights = jax.random.uniform(jax.random.fold_in(jax.random.fold_in(rng, 6), position), (shards_of,), jnp.float32, low / len(pieces), largest / len(pieces))
        return jnp.repeat(jnp.exp(heights), shape[position] // shards_of).reshape((-1,) + (1,) * (len(shape) - position - 1))

    loudness = one(*pieces[0])
    for cut in pieces[1:]:
        loudness = loudness * one(*cut)
    return loudness


def gaussian(own_key, shape, width, bound, cuts=(), kind=jnp.bfloat16):
    drawn = jax.random.normal(own_key, shape, jnp.float32) * width
    if len(cuts) > 0:
        drawn = block_scale(own_key, shape, cuts, -0.22, 0.18) * drawn
    return jnp.clip(drawn, min=-bound, max=bound).astype(kind)


def setup_inputs(seed: int = 0) -> dict:
    arg_keys = jax.random.split(jax.random.key(seed), 5)
    recording = gaussian(arg_keys[0], (SAMPLES, C), 1.0, 6.0, ((0, 128),))
    spike_times = draw_spike_times(jax.random.fold_in(arg_keys[4], 71), 0)
    unit_labels = draw_unit_labels(jax.random.fold_in(arg_keys[4], 71), 0)
    old_templates = gaussian(arg_keys[3], (UNITS, FEAT), 0.5, 3.0, ((0, 8),))
    return dict(recording=recording, spike_times=spike_times, unit_labels=unit_labels, old_templates=old_templates)


def reference(recording, spike_times, unit_labels, old_templates):
    feat = C * TAPS

    def add_one(i, carry):
        sums, counts = carry
        start = (spike_times[i] - HALF).astype(jnp.int32)
        snip = lax.dynamic_slice(recording, (start, jnp.int32(0)), (TAPS, C))
        row = snip.T.reshape(1, feat).astype(jnp.float32)
        label = unit_labels[i].astype(jnp.int32)
        current = lax.dynamic_slice(sums, (label, jnp.int32(0)), (1, feat))
        sums = lax.dynamic_update_slice(sums, current + row, (label, jnp.int32(0)))
        counts = counts.at[label].add(jnp.float32(1.0))
        return (sums, counts)
    sums0 = jnp.zeros((UNITS, feat), jnp.float32)
    counts0 = jnp.zeros((UNITS,), jnp.float32)
    sums, counts = lax.fori_loop(0, SPIKES, add_one, (sums0, counts0))
    weight = counts / (counts + 4.0)
    mean = sums / jnp.maximum(counts, 1.0)[:, None]
    old = old_templates.astype(jnp.float32)
    templates = (old + weight[:, None] * (mean - old)).astype(jnp.bfloat16)
    extended = jnp.concatenate([recording, jnp.zeros((TAPS - 1, C), jnp.bfloat16)], axis=0)
    signal = extended.astype(jnp.float32)[None]
    kernels = templates.astype(jnp.float32).reshape(OWNERS, PANEL, C, TAPS)

    def one_panel(kernel):
        out = lax.conv_general_dilated(signal, kernel, (STRIDE,), 'VALID', dimension_numbers=('NWC', 'OIW', 'NCW'), precision=lax.Precision.HIGHEST)
        return out[0]
    scores = lax.map(one_panel, kernels).reshape(UNITS, WINDOWS)
    scores = scores * (1.0 / jnp.sqrt(jnp.float32(feat)))
    return (templates, scores)
```

```python
import functools

import jax
import jax.numpy as jnp
from jax import lax
from jax.experimental import pallas as pl
from jax.experimental.pallas import tpu as pltpu
from jax.sharding import PartitionSpec as P

MESH = pl.DeviceIdType.MESH
TAPS = 61
CAP = 8
GROUPS = 4
STEP = 16
PHASES = 8
LINES = 128
ROWS = 1056
TAIL = 16
CHUNKS = 3
WIDE = 128
FLAT = STEP + 1


def dot_f32(a, b):
    return jnp.dot(a, b, preferred_element_type=jnp.float32)


def dot_nt(a, b):
    return lax.dot_general(a, b, (((1,), (1,)), ((), ())), preferred_element_type=jnp.float32)


def exchange_kernel(
    own_ref,
    tab_ref,
    old_ref,
    x_ref,
    t_ref,
    v_ref,
    tabs,
    picks,
    snip,
    sums,
    away,
    swap_in,
    part,
    part_in,
    tab_s,
    tab_r,
    ag_s,
    ag_r,
    halo_s,
    halo_r,
    swap_s,
    swap_r,
    rs_s,
    rs_r,
    tg_s,
    tg_r,
    fw_s,
    fw_r,
):
    t = lax.axis_index("tm")
    u = lax.axis_index("unit")
    core = lax.rem(t, 2)
    chip = t // 2
    z = lax.rem(u, 4)
    side = u - z
    other = 4 - side
    zp = lax.rem(z + 1, 4)
    zm = lax.rem(z + 3, 4)
    zo = lax.rem(z + 2, 4)
    up, down, across = side + zp, side + zm, other + z

    barrier = pltpu.get_barrier_semaphore()
    for rel in range(1, 8):
        pl.semaphore_signal(
            barrier, inc=1, device_id={"unit": lax.rem(u + rel, 8)}, device_id_type=MESH
        )
    for rel in range(1, 16):
        pl.semaphore_signal(
            barrier, inc=1, device_id={"tm": lax.rem(t + rel, 16)}, device_id_type=MESH
        )
    pl.semaphore_wait(barrier, 22)

    tab_cp = []
    for rel in range(1, 8):
        to = lax.rem(u + rel, 8)
        c = pltpu.make_async_remote_copy(
            src_ref=tab_ref.at[to],
            dst_ref=tabs.at[u],
            send_sem=tab_s.at[rel - 1],
            recv_sem=tab_r.at[rel - 1],
            device_id={"unit": to},
            device_id_type=MESH,
        )
        c.start()
        tab_cp.append(c)

    row = lax.broadcasted_iota(jnp.int32, (LINES, 1024), 0) * PHASES
    col = lax.broadcasted_iota(jnp.int32, (LINES, 1024), 1)
    mine = pl.ds(pl.multiple_of(u * LINES, LINES), LINES)
    own = own_ref[...]
    for p in range(PHASES):
        pick = jnp.where(col == row + p, 1.0, 0.0).astype(jnp.bfloat16)
        got = dot_f32(pick, own).astype(jnp.bfloat16)
        for cc in range(CHUNKS):
            lane = (cc * PHASES + p) * WIDE
            x_ref[mine, lane : lane + WIDE] = got[:, cc * WIDE : (cc + 1) * WIDE]

    def block(index, cc, first=0, count=LINES):
        return x_ref.at[
            pl.ds(pl.multiple_of(index * LINES + first, 16), count),
            cc * PHASES * WIDE : (cc + 1) * PHASES * WIDE,
        ]

    def hop(cc, k, ref, to):
        return pltpu.make_async_remote_copy(
            src_ref=ref,
            dst_ref=ref,
            send_sem=ag_s.at[cc * 8 + k],
            recv_sem=ag_r.at[cc * 8 + k],
            device_id={"unit": to},
            device_id_type=MESH,
        )

    half = LINES // 2
    hops = []
    for cc in range(CHUNKS):
        hops.append(
            [
                hop(cc, 0, block(u, cc), across),
                hop(cc, 1, block(u, cc), up),
                hop(cc, 2, block(u, cc), down),
                hop(cc, 3, block(down, cc, 0, half), up),
                hop(cc, 4, block(up, cc, half, half), down),
                hop(cc, 5, block(across, cc), up),
                hop(cc, 6, block(across, cc), down),
                hop(cc, 7, block(side + zo, cc), across),
            ]
        )

    def own_sends(cc):
        for k in (0, 1, 2):
            hops[cc][k].start()

    def forward_one(cc):
        hops[cc][0].wait_recv()
        hops[cc][5].start()
        hops[cc][6].start()
        hops[cc][1].wait_recv()
        hops[cc][3].start()
        hops[cc][2].wait_recv()
        hops[cc][4].start()

    def forward_two(cc):
        hops[cc][3].wait_recv()
        hops[cc][4].wait_recv()
        hops[cc][7].start()

    def finish(cc):
        hops[cc][5].wait_recv()
        hops[cc][6].wait_recv()
        hops[cc][7].wait_recv()

    own_sends(0)

    tabs[u] = tab_ref[u]
    for c in tab_cp:
        c.wait_recv()

    tval = lax.broadcasted_iota(jnp.int32, (CAP, 1024), 1)
    tval = (tval % LINES) * PHASES + tval // LINES
    lead = lax.broadcasted_iota(jnp.int32, (GROUPS * STEP, 1, 1), 0)
    tap = (lead % GROUPS) * STEP + lead // GROUPS
    tap = jnp.where(tap < TAPS, tap, -100000)
    order = [u, across, up, down, side + zo, other + zp, other + zm, other + zo]

    def build_picks(i, carry):
        start = tabs[i][:, 0:1]
        gap = (tval - start)[None]
        pick = jnp.where(gap == tap, 1.0, 0.0).reshape(GROUPS * STEP * CAP, 1024)
        picks[i] = pick.astype(jnp.bfloat16)
        return carry

    lax.fori_loop(0, 8, build_picks, 0)

    labels = tabs[...].reshape(64, 128)[:, 64:65]
    labels = jnp.concatenate([labels] * GROUPS, axis=0)
    r4 = lax.broadcasted_iota(jnp.int32, (256, 256), 0)
    c4 = lax.broadcasted_iota(jnp.int32, (256, 256), 1)
    merge = jnp.where(
        jnp.logical_and(labels == c4 % 64, r4 // 64 == c4 // 64), 1.0, 0.0
    )
    merge = merge.T.astype(jnp.bfloat16)
    tally = dot_f32(merge, jnp.ones((256, WIDE), jnp.bfloat16))

    def gather(cc, position):
        b = order[position]
        base = cc * PHASES * WIDE
        rows = pl.ds(pl.multiple_of(b * LINES, LINES), LINES)
        data = jnp.concatenate(
            [x_ref[rows, base + p * WIDE : base + (p + 1) * WIDE] for p in range(PHASES)],
            axis=0,
        )
        cut = dot_f32(picks[b], data)
        at = pl.ds(pl.multiple_of(b * CAP, CAP), CAP)
        for j in range(STEP):
            for g in range(GROUPS):
                r = (j * GROUPS + g) * CAP
                snip[g, at, j * WIDE : (j + 1) * WIDE] = cut[r : r + CAP]

    def halo(cc):
        lanes = pl.ds(cc * PHASES * WIDE, PHASES * WIDE)
        return pltpu.make_async_remote_copy(
            src_ref=x_ref.at[pl.ds(0, TAIL), lanes],
            dst_ref=x_ref.at[pl.ds(1024, TAIL), lanes],
            send_sem=halo_s.at[cc],
            recv_sem=halo_r.at[cc],
            device_id={"tm": lax.rem(t + 15, 16)},
            device_id_type=MESH,
        )

    halos = [halo(cc) for cc in range(CHUNKS)]

    def swap(cc):
        return pltpu.make_async_remote_copy(
            src_ref=away.at[cc],
            dst_ref=swap_in.at[cc],
            send_sem=swap_s.at[cc],
            recv_sem=swap_r.at[cc],
            device_id={"tm": chip * 2 + 1 - core},
            device_id_type=MESH,
        )

    swaps = [swap(cc) for cc in range(CHUNKS)]

    def merge_labels(cc):
        out = dot_f32(merge, snip[...].reshape(256, STEP * WIDE).astype(jnp.bfloat16))
        out = jnp.concatenate([out, tally], axis=1).reshape(8, 2, 16, FLAT * WIDE)
        sums[cc] = out
        away[cc] = sums[cc, :, 1 - core].astype(jnp.bfloat16)
        swaps[cc].start()

    def scatter(cc, rel):
        to = lax.rem(chip + rel, 8)
        return pltpu.make_async_remote_copy(
            src_ref=part.at[cc, to],
            dst_ref=part_in.at[cc, rel - 1],
            send_sem=rs_s.at[cc * 7 + rel - 1],
            recv_sem=rs_r.at[cc * 7 + rel - 1],
            device_id={"tm": to * 2 + core},
            device_id_type=MESH,
        )

    scatters = [[scatter(cc, rel) for rel in range(1, 8)] for cc in range(CHUNKS)]

    def reduce_start(cc):
        swaps[cc].wait_recv()
        part[cc] = (sums[cc, :, core] + swap_in[cc].astype(jnp.float32)).astype(jnp.bfloat16)
        for c in scatters[cc]:
            c.start()

    def panel(cc, ch, co):
        return t_ref.at[ch, co, :, cc * STEP * WIDE : (cc + 1) * STEP * WIDE]

    def give(cc, rel):
        return pltpu.make_async_remote_copy(
            src_ref=panel(cc, chip, core),
            dst_ref=panel(cc, chip, core),
            send_sem=tg_s.at[cc * 7 + rel - 1],
            recv_sem=tg_r.at[cc * 7 + rel - 1],
            device_id={"tm": lax.rem(chip + rel, 8) * 2 + core},
            device_id_type=MESH,
        )

    def pass_on(cc, rel):
        ch = lax.rem(chip + 8 - rel, 8)
        return pltpu.make_async_remote_copy(
            src_ref=panel(cc, ch, core),
            dst_ref=panel(cc, ch, core),
            send_sem=fw_s.at[cc * 8 + rel],
            recv_sem=fw_r.at[cc * 8 + rel],
            device_id={"tm": chip * 2 + 1 - core},
            device_id_type=MESH,
        )

    gives = [[give(cc, rel) for rel in range(1, 8)] for cc in range(CHUNKS)]
    passes = [[pass_on(cc, rel) for rel in range(8)] for cc in range(CHUNKS)]

    def refine(cc):
        for c in scatters[cc]:
            c.wait_recv()
        total = sums[cc, chip, core] + swap_in[cc, chip].astype(jnp.float32)
        for rel in range(7):
            total = total + part_in[cc, rel].astype(jnp.float32)
        counts = total[:, STEP * WIDE :]
        weight = counts / (counts + 4.0)
        safe = jnp.maximum(counts, 1.0)
        old = old_ref[cc].astype(jnp.float32)
        fresh = []
        for j in range(STEP):
            lanes = slice(j * WIDE, (j + 1) * WIDE)
            base = old[:, lanes]
            fresh.append(base + weight * (total[:, lanes] / safe - base))
        t_ref[chip, core, :, cc * STEP * WIDE : (cc + 1) * STEP * WIDE] = jnp.concatenate(
            fresh, axis=1
        ).astype(jnp.bfloat16)
        for c in gives[cc]:
            c.start()
        passes[cc][0].start()

    def spread(cc):
        for rel in range(1, 8):
            gives[cc][rel - 1].wait_recv()
            passes[cc][rel].start()

    def settle(cc):
        for c in passes[cc]:
            c.wait_recv()

    for cc in range(CHUNKS):
        gather(cc, 0)
        forward_one(cc)
        if cc + 1 < CHUNKS:
            own_sends(cc + 1)
        gather(cc, 1)
        gather(cc, 2)
        gather(cc, 3)
        if cc >= 1:
            refine(cc - 1)
        forward_two(cc)
        gather(cc, 4)
        finish(cc)
        halos[cc].start()
        gather(cc, 5)
        gather(cc, 6)
        gather(cc, 7)
        merge_labels(cc)
        if cc >= 1:
            spread(cc - 1)
        reduce_start(cc)
    refine(CHUNKS - 1)
    spread(CHUNKS - 1)
    for cc in range(CHUNKS):
        settle(cc)
        halos[cc].wait_recv()

    @pl.when(t == 15)
    def _():
        x_ref[1024 : 1024 + TAIL, :] = jnp.zeros((TAIL, x_ref.shape[1]), jnp.bfloat16)

    want = lax.broadcasted_iota(jnp.int32, (WIDE, 128), 0) - t * 24
    place = lax.broadcasted_iota(jnp.int32, (WIDE, 128), 1)
    chosen = [
        jnp.where(jnp.logical_and(want + cc * WIDE == place, place < 24), 1.0, 0.0).astype(
            jnp.bfloat16
        )
        for cc in range(CHUNKS)
    ]
    for j in range(STEP):
        acc = None
        for cc in range(CHUNKS):
            lane = (cc * STEP + j) * WIDE
            piece = t_ref[:, :, :, lane : lane + WIDE].reshape(256, WIDE)
            piece = dot_f32(piece, chosen[cc])
            acc = piece if acc is None else acc + piece
        v_ref[j] = acc.astype(jnp.bfloat16)

    for c in tab_cp:
        c.wait_send()
    for cc in range(CHUNKS):
        for c in hops[cc] + [halos[cc], swaps[cc]] + scatters[cc] + gives[cc] + passes[cc]:
            c.wait_send()


def exchange(own, tab, old):
    bf16, f32 = jnp.bfloat16, jnp.float32
    dma = pltpu.SemaphoreType.DMA
    vmem = pl.BlockSpec(memory_space=pltpu.VMEM)
    return pl.pallas_call(
        exchange_kernel,
        out_shape=(
            jax.ShapeDtypeStruct((ROWS, CHUNKS * PHASES * WIDE), bf16),
            jax.ShapeDtypeStruct((8, 2, 16, CHUNKS * STEP * WIDE), bf16),
            jax.ShapeDtypeStruct((STEP, 256, 128), bf16),
        ),
        in_specs=[vmem] * 3,
        out_specs=[vmem] * 3,
        scratch_shapes=[
            pltpu.VMEM((8, CAP, 128), jnp.int32),
            pltpu.VMEM((8, GROUPS * STEP * CAP, 1024), bf16),
            pltpu.VMEM((GROUPS, 64, STEP * WIDE), f32),
            pltpu.VMEM((CHUNKS, 8, 2, 16, FLAT * WIDE), f32),
            pltpu.VMEM((CHUNKS, 8, 16, FLAT * WIDE), bf16),
            pltpu.VMEM((CHUNKS, 8, 16, FLAT * WIDE), bf16),
            pltpu.VMEM((CHUNKS, 8, 16, FLAT * WIDE), bf16),
            pltpu.VMEM((CHUNKS, 7, 16, FLAT * WIDE), bf16),
            dma((7,)),
            dma((7,)),
            dma((CHUNKS * 8,)),
            dma((CHUNKS * 8,)),
            dma((CHUNKS,)),
            dma((CHUNKS,)),
            dma((CHUNKS,)),
            dma((CHUNKS,)),
            dma((CHUNKS * 7,)),
            dma((CHUNKS * 7,)),
            dma((CHUNKS * 7,)),
            dma((CHUNKS * 7,)),
            dma((CHUNKS * 8,)),
            dma((CHUNKS * 8,)),
        ],
        compiler_params=pltpu.CompilerParams(
            collective_id=0, has_side_effects=True, vmem_limit_bytes=56 << 20
        ),
        name="exchange",
    )(own, tab, old)


def correlate_kernel(scale, x_ref, t_ref, out_ref, y_ref, rows_ref):
    size = ROWS // 2
    for d in range(4):

        def one(i, carry):
            first = pl.multiple_of(i * size, 16)
            for e in range(3):
                low = max(0, 8 * e - 2 * d)
                high = min(STEP, 8 * e + 8 - 2 * d)
                if low >= high:
                    continue
                total = None
                for cc in range(CHUNKS):
                    p = 2 * d + low - 8 * e
                    xl = (cc * PHASES + p) * WIDE
                    tl = (cc * STEP + low) * WIDE
                    span = (high - low) * WIDE
                    part = dot_nt(
                        x_ref[pl.ds(first, size), xl : xl + span], t_ref[:, tl : tl + span]
                    )
                    total = part if total is None else total + part
                y_ref[e, pl.ds(first, size), :] = total
            return carry

        lax.fori_loop(0, 2, one, 0)
        a = y_ref[0, 0:1032, 0:128] + y_ref[0, 4 : 4 + 1032, 128:256]
        for e in (1, 2) if d > 0 else (1,):
            a = a + y_ref[e, e : e + 1032, 0:128] + y_ref[e, e + 4 : e + 4 + 1032, 128:256]
        f = a[0:1024, 0:64] + a[2 : 2 + 1024, 64:128]
        rows_ref[pl.ds(d, 1024, stride=4), 0:64] = f * scale
    out_ref[...] = rows_ref[...].T[0:64]


def correlate(x, t2, scale):
    vmem = pl.BlockSpec(memory_space=pltpu.VMEM)
    return pl.pallas_call(
        functools.partial(correlate_kernel, scale),
        out_shape=jax.ShapeDtypeStruct((64, 4096), jnp.float32),
        in_specs=[vmem] * 2,
        out_specs=vmem,
        scratch_shapes=[
            pltpu.VMEM((3, ROWS, 256), jnp.float32),
            pltpu.VMEM((4096, 128), jnp.float32),
        ],
        compiler_params=pltpu.CompilerParams(vmem_limit_bytes=48 << 20),
        name="correlate",
    )(x, t2)


def body(recording, spike_times, unit_labels, old_templates):
    sub_rows, chans = recording.shape
    panel, feat = old_templates.shape
    spikes = spike_times.shape[0]
    t = lax.axis_index("tm")
    u = lax.axis_index("unit")
    start = spike_times - (t * 8 + u) * sub_rows - (TAPS - 1) // 2
    owner = unit_labels // panel
    within = unit_labels % panel
    before = jnp.arange(spikes)[None, :] < jnp.arange(spikes)[:, None]
    rank = jnp.sum(
        jnp.logical_and(owner[:, None] == owner[None, :], before).astype(jnp.int32), axis=1
    )
    slot = owner * CAP + rank
    hit = jnp.arange(8 * CAP)[:, None] == slot[None, :]
    start_of = jnp.sum(jnp.where(hit, start[None, :], 0), axis=1)
    label_of = jnp.sum(jnp.where(hit, within[None, :] + 1, 0), axis=1) - 1
    lane = jnp.arange(128)[None, :]
    tab = jnp.where(lane < 64, start_of[:, None], label_of[:, None]).reshape(8, CAP, 128)

    rows = lax.dynamic_slice_in_dim(old_templates, (t % 4) * 16, 16, 0)
    rows = rows.reshape(16, chans, TAPS)
    rows = jnp.pad(rows, ((0, 0), (0, 0), (0, GROUPS * STEP - TAPS)))
    rows = lax.dynamic_slice_in_dim(rows, (t // 4) * STEP, STEP, 2)
    old = rows.reshape(16, CHUNKS, WIDE, STEP).transpose(1, 0, 3, 2)
    old = old.reshape(CHUNKS, 16, STEP * WIDE)

    x, t2, v = exchange(recording, tab.astype(jnp.int32), old)
    scale = 1.0 / (feat**0.5)
    scores = correlate(x, t2.reshape(256, CHUNKS * STEP * WIDE), scale)
    share = chans // 16
    v = v[:, :, :share].reshape(STEP, GROUPS, panel, share).transpose(2, 3, 1, 0)
    templates = v.reshape(panel, share, GROUPS * STEP)[:, :, :TAPS].reshape(panel, share * TAPS)
    return (templates, scores)


def solution(mesh):
    in_specs = (P(("tm", "unit"), None), P(("tm", "unit")), P(("tm", "unit")), P("unit", None))
    out_specs = (P("unit", "tm"), P("unit", "tm"))
    return jax.shard_map(body, mesh=mesh, in_specs=in_specs, out_specs=out_specs, check_vma=False)
```

```python
import functools

import jax
import jax.numpy as jnp
from jax import lax
from jax.experimental import pallas as pl
from jax.experimental.pallas import tpu as pltpu
from jax.sharding import PartitionSpec as P

MESH = pl.DeviceIdType.MESH
TAPS = 61
CAP = 8
GROUPS = 4
STEP = 16
PHASES = 8
LINES = 128
ROWS = 1056
TAIL = 16
CHUNKS = 3
WIDE = 128
FLAT = STEP + 1
SIZE = ROWS // 2
LONG = TAPS * WIDE


def dot_f32(a, b):
    return jnp.dot(a, b, preferred_element_type=jnp.float32)


def dot_nt(a, b):
    return lax.dot_general(a, b, (((1,), (1,)), ((), ())), preferred_element_type=jnp.float32)


PLANES = [(d, e) for d in range(4) for e in range(3 if d > 0 else 2)]


def refine_kernel(
    scale,
    own_ref,
    tab_ref,
    old_ref,
    new_ref,
    score_ref,
    x_ref,
    t_ref,
    old_rows,
    old_tall,
    old_wide,
    tabs,
    picks,
    snip,
    sums,
    away,
    swap_in,
    part,
    part_in,
    keep,
    side_out,
    side_in,
    y_ref,
    rows_ref,
    new_tall,
    old_s,
    tab_s,
    tab_r,
    ag_s,
    ag_r,
    halo_s,
    halo_r,
    swap_s,
    swap_r,
    ys_s,
    ys_r,
    xs_s,
    xs_r,
    xg_s,
    xg_r,
    yg_s,
    yg_r,
    fw_s,
    fw_r,
):
    t = lax.axis_index("tm")
    u = lax.axis_index("unit")
    core = lax.rem(t, 2)
    chip = t // 2
    yy = chip // 2
    xh = lax.rem(chip, 2)
    beside = yy * 2 + 1 - xh
    z = lax.rem(u, 4)
    side = u - z
    other = 4 - side
    zp = lax.rem(z + 1, 4)
    zm = lax.rem(z + 3, 4)
    zo = lax.rem(z + 2, 4)
    up, down, across = side + zp, side + zm, other + z

    ug = lax.rem(t, 4)
    tg = t // 4
    old_cp = pltpu.make_async_copy(
        old_ref.at[pl.ds(pl.multiple_of(ug * 16, 16), 16)], old_rows, old_s
    )
    old_cp.start()

    barrier = pltpu.get_barrier_semaphore()
    for rel in range(1, 8):
        pl.semaphore_signal(
            barrier, inc=1, device_id={"unit": lax.rem(u + rel, 8)}, device_id_type=MESH
        )
    for rel in range(1, 16):
        pl.semaphore_signal(
            barrier, inc=1, device_id={"tm": lax.rem(t + rel, 16)}, device_id_type=MESH
        )
    pl.semaphore_wait(barrier, 22)

    row = lax.broadcasted_iota(jnp.int32, (LINES, 1024), 0) * PHASES
    col = lax.broadcasted_iota(jnp.int32, (LINES, 1024), 1)
    mine = pl.ds(pl.multiple_of(u * LINES, LINES), LINES)

    def sort_phases(first, last):
        own = own_ref[:, first * WIDE : last * WIDE]
        for p in range(PHASES):
            pick = jnp.where(col == row + p, 1.0, 0.0).astype(jnp.bfloat16)
            got = dot_f32(pick, own).astype(jnp.bfloat16)
            for cc in range(first, last):
                lane = (cc * PHASES + p) * WIDE
                x_ref[mine, lane : lane + WIDE] = got[
                    :, (cc - first) * WIDE : (cc - first + 1) * WIDE
                ]

    def block(index, cc, first=0, count=LINES):
        return x_ref.at[
            pl.ds(pl.multiple_of(index * LINES + first, 16), count),
            cc * PHASES * WIDE : (cc + 1) * PHASES * WIDE,
        ]

    def remote(src, dst, send, recv, where):
        return pltpu.make_async_remote_copy(
            src_ref=src,
            dst_ref=dst,
            send_sem=send,
            recv_sem=recv,
            device_id=where,
            device_id_type=MESH,
        )

    def hop(cc, k, ref, to):
        return remote(ref, ref, ag_s.at[cc * 8 + k], ag_r.at[cc * 8 + k], {"unit": to})

    half = LINES // 2
    hops = [
        [
            hop(cc, 0, block(u, cc), across),
            hop(cc, 1, block(u, cc), up),
            hop(cc, 2, block(u, cc), down),
            hop(cc, 3, block(down, cc, 0, half), up),
            hop(cc, 4, block(up, cc, half, half), down),
            hop(cc, 5, block(across, cc), up),
            hop(cc, 6, block(across, cc), down),
            hop(cc, 7, block(side + zo, cc), across),
        ]
        for cc in range(CHUNKS)
    ]

    def own_sends(cc):
        for k in (0, 1, 2):
            hops[cc][k].start()

    def forward_one(cc):
        hops[cc][0].wait_recv()
        hops[cc][5].start()
        hops[cc][6].start()
        hops[cc][1].wait_recv()
        hops[cc][3].start()
        hops[cc][2].wait_recv()
        hops[cc][4].start()

    def forward_two(cc):
        hops[cc][3].wait_recv()
        hops[cc][4].wait_recv()
        hops[cc][7].start()

    def finish(cc):
        hops[cc][5].wait_recv()
        hops[cc][6].wait_recv()
        hops[cc][7].wait_recv()
        halos[cc].start()

    def halo(cc):
        lanes = pl.ds(cc * PHASES * WIDE, PHASES * WIDE)
        return remote(
            x_ref.at[pl.ds(0, TAIL), lanes],
            x_ref.at[pl.ds(1024, TAIL), lanes],
            halo_s.at[cc],
            halo_r.at[cc],
            {"tm": lax.rem(t + 15, 16)},
        )

    halos = [halo(cc) for cc in range(CHUNKS)]

    sort_phases(0, 1)
    own_sends(0)
    tab_cp = []
    for rel in range(1, 8):
        to = lax.rem(u + rel, 8)
        c = remote(
            tab_ref.at[to], tabs.at[u], tab_s.at[rel - 1], tab_r.at[rel - 1], {"unit": to}
        )
        c.start()
        tab_cp.append(c)
    sort_phases(1, CHUNKS)
    tabs[u] = tab_ref[u]
    for c in tab_cp:
        c.wait_recv()

    tval = lax.broadcasted_iota(jnp.int32, (CAP, 1024), 1)
    tval = (tval % LINES) * PHASES + tval // LINES
    lead = lax.broadcasted_iota(jnp.int32, (GROUPS * STEP, 1, 1), 0)
    tap = (lead % GROUPS) * STEP + lead // GROUPS
    tap = jnp.where(tap < TAPS, tap, -100000)
    order = [u, across, up, down, side + zo, other + zp, other + zm, other + zo]

    def build_picks(i, carry):
        start = tabs[i][:, 0:1]
        gap = (tval - start)[None]
        pick = jnp.where(gap == tap, 1.0, 0.0).reshape(GROUPS * STEP * CAP, 1024)
        picks[i] = pick.astype(jnp.bfloat16)
        return carry

    lax.fori_loop(0, 8, build_picks, 0)

    labels = tabs[...].reshape(64, 128)[:, 64:65]
    labels = jnp.concatenate([labels] * GROUPS, axis=0)
    r4 = lax.broadcasted_iota(jnp.int32, (256, 256), 0)
    c4 = lax.broadcasted_iota(jnp.int32, (256, 256), 1)
    merge = jnp.where(
        jnp.logical_and(labels == c4 % 64, r4 // 64 == c4 // 64), 1.0, 0.0
    )
    merge = merge.T.astype(jnp.bfloat16)
    tally = dot_f32(merge, jnp.ones((256, WIDE), jnp.bfloat16))

    def relay_old():
        old_cp.wait()
        for cc in range(CHUNKS):

            def turn(i, carry):
                src = pl.ds(pl.multiple_of(cc * LONG + i * 128, 128), 128)
                at = pl.ds(pl.multiple_of(i * 128, 128), 128)
                old_tall[at, :] = old_rows[:, src].astype(jnp.float32).T
                return carry

            lax.fori_loop(0, TAPS, turn, 0)
            for j in range(STEP):
                piece = old_tall[pl.ds(tg * STEP + j, WIDE, stride=TAPS), :].T
                piece = jnp.where(tg * STEP + j < TAPS, piece, 0.0)
                old_wide[cc, :, j * WIDE : (j + 1) * WIDE] = piece

    def gather(cc, position):
        b = order[position]
        base = cc * PHASES * WIDE
        rows = pl.ds(pl.multiple_of(b * LINES, LINES), LINES)
        data = jnp.concatenate(
            [x_ref[rows, base + p * WIDE : base + (p + 1) * WIDE] for p in range(PHASES)],
            axis=0,
        )
        cut = dot_f32(picks[b], data)
        at = pl.ds(pl.multiple_of(b * CAP, CAP), CAP)
        for j in range(STEP):
            for g in range(GROUPS):
                r = (j * GROUPS + g) * CAP
                snip[g, at, j * WIDE : (j + 1) * WIDE] = cut[r : r + CAP]

    swaps = [
        remote(away, swap_in.at[cc], swap_s.at[cc], swap_r.at[cc], {"tm": chip * 2 + 1 - core})
        for cc in range(CHUNKS)
    ]

    def merge_labels(cc):
        if cc > 0:
            swaps[cc - 1].wait_send()
        out = dot_f32(merge, snip[...].reshape(256, STEP * WIDE).astype(jnp.bfloat16))
        out = jnp.concatenate([out, tally], axis=1).reshape(4, 2, 2, 16, FLAT * WIDE)
        sums[...] = out
        away[...] = sums[:, :, 1 - core]
        swaps[cc].start()

    def y_send(cc, rel):
        to = lax.rem(yy + rel, 4)
        return remote(
            part.at[cc, to],
            part_in.at[cc, rel - 1],
            ys_s.at[cc * 3 + rel - 1],
            ys_r.at[cc * 3 + rel - 1],
            {"tm": (to * 2 + xh) * 2 + core},
        )

    y_sends = [[y_send(cc, rel) for rel in (1, 2, 3)] for cc in range(CHUNKS)]
    x_sends = [
        remote(side_out.at[cc], side_in.at[cc], xs_s.at[cc], xs_r.at[cc], {"tm": beside * 2 + core})
        for cc in range(CHUNKS)
    ]

    def reduce_one(cc):
        swaps[cc].wait_recv()
        both = sums[:, :, core] + swap_in[cc]
        part[cc] = both.astype(jnp.bfloat16)
        for c in y_sends[cc]:
            c.start()
        sums[:, :, core] = both

    def reduce_two(cc):
        for c in y_sends[cc]:
            c.wait_recv()
        far = sums[yy, 1 - xh, core]
        near = sums[yy, xh, core]
        for rel in range(3):
            far = far + part_in[cc, rel, 1 - xh].astype(jnp.float32)
            near = near + part_in[cc, rel, xh].astype(jnp.float32)
        side_out[cc] = far.astype(jnp.bfloat16)
        x_sends[cc].start()
        keep[cc] = near

    def panel(cc, ch, co):
        return t_ref.at[ch, co, :, cc * STEP * WIDE : (cc + 1) * STEP * WIDE]

    def x_give(cc):
        ref = panel(cc, chip, core)
        return remote(ref, ref, xg_s.at[cc], xg_r.at[cc], {"tm": beside * 2 + core})

    def y_give(cc, rel, ch, k):
        ref = panel(cc, ch, core)
        to = lax.rem(yy + rel, 4)
        return remote(
            ref,
            ref,
            yg_s.at[cc * 6 + k * 3 + rel - 1],
            yg_r.at[cc * 6 + k * 3 + rel - 1],
            {"tm": (to * 2 + xh) * 2 + core},
        )

    def pass_on(cc, k, ch):
        ref = panel(cc, ch, core)
        return remote(
            ref, ref, fw_s.at[cc * 8 + k], fw_r.at[cc * 8 + k], {"tm": chip * 2 + 1 - core}
        )

    x_gives = [x_give(cc) for cc in range(CHUNKS)]
    y_gives = [
        [y_give(cc, rel, ch, k) for k, ch in ((0, chip), (1, beside)) for rel in (1, 2, 3)]
        for cc in range(CHUNKS)
    ]
    origin = [chip, beside]
    for half_x in (xh, 1 - xh):
        for rel in (1, 2, 3):
            origin.append(lax.rem(yy + 4 - rel, 4) * 2 + half_x)
    passes = [[pass_on(cc, k, origin[k]) for k in range(8)] for cc in range(CHUNKS)]

    def refine(cc):
        x_sends[cc].wait_recv()
        total = keep[cc] + side_in[cc].astype(jnp.float32)
        counts = total[:, STEP * WIDE :]
        weight = counts / (counts + 4.0)
        safe = jnp.maximum(counts, 1.0)
        fresh = []
        for j in range(STEP):
            lanes = slice(j * WIDE, (j + 1) * WIDE)
            base = old_wide[cc, :, lanes]
            fresh.append(base + weight * (total[:, lanes] / safe - base))
        t_ref[chip, core, :, cc * STEP * WIDE : (cc + 1) * STEP * WIDE] = jnp.concatenate(
            fresh, axis=1
        ).astype(jnp.bfloat16)
        x_gives[cc].start()
        for c in y_gives[cc][:3]:
            c.start()
        passes[cc][0].start()

    def spread_one(cc):
        x_gives[cc].wait_recv()
        for c in y_gives[cc][3:]:
            c.start()
        passes[cc][1].start()

    def spread_two(cc):
        for k in range(6):
            y_gives[cc][k].wait_recv()
            passes[cc][2 + k].start()

    def settle(cc):
        for c in passes[cc]:
            c.wait_recv()
        halos[cc].wait_recv()

        @pl.when(t == 15)
        def _():
            x_ref[1024 : 1024 + TAIL, cc * PHASES * WIDE : (cc + 1) * PHASES * WIDE] = jnp.zeros(
                (TAIL, PHASES * WIDE), jnp.bfloat16
            )

    def correlate(cc, d):
        def one(i, carry):
            first = pl.multiple_of(i * SIZE, 16)
            for at, (dd, e) in enumerate(PLANES):
                if dd != d:
                    continue
                low = max(0, 8 * e - 2 * d)
                high = min(STEP, 8 * e + 8 - 2 * d)
                xl = (cc * PHASES + 2 * d + low - 8 * e) * WIDE
                tl = (cc * STEP + low) * WIDE
                span = (high - low) * WIDE
                panels = t_ref[:, :, :, tl : tl + span].reshape(256, span)
                total = dot_nt(x_ref[pl.ds(first, SIZE), xl : xl + span], panels)
                if cc == 0:
                    y_ref[at, pl.ds(first, SIZE), :] = total
                else:
                    y_ref[at, pl.ds(first, SIZE), :] += total
            return carry

        lax.fori_loop(0, 2, one, 0)

    def collect(d):
        a = None
        for at, (dd, e) in enumerate(PLANES):
            if dd != d:
                continue
            b = y_ref[at, e : e + 1032, 0:128] + y_ref[at, e + 4 : e + 4 + 1032, 128:256]
            a = b if a is None else a + b
        f = a[0:1024, 0:64] + a[2 : 2 + 1024, 64:128]
        rows_ref[pl.ds(d, 1024, stride=4), 0:64] = f * scale

    def write_new():
        want = lax.broadcasted_iota(jnp.int32, (32, WIDE), 1) - t * 24
        place = lax.broadcasted_iota(jnp.int32, (32, WIDE), 0)
        chosen = [
            jnp.where(jnp.logical_and(want + cc * WIDE == place, place < 24), 1.0, 0.0).astype(
                jnp.bfloat16
            )
            for cc in range(CHUNKS)
        ]
        for j in range(STEP):
            acc = None
            for cc in range(CHUNKS):
                lane = (cc * STEP + j) * WIDE
                piece = t_ref[:, :, :, lane : lane + WIDE].reshape(256, WIDE)
                piece = dot_nt(chosen[cc], piece)
                acc = piece if acc is None else acc + piece
            for g in range(GROUPS):
                if g * STEP + j < TAPS:
                    new_tall[pl.ds(g * STEP + j, 24, stride=TAPS), 0:64] = acc[
                        0:24, g * 64 : (g + 1) * 64
                    ]
        new_ref[...] = new_tall[...].T[0:64, 0 : 24 * TAPS].astype(jnp.bfloat16)

    relay_old()

    forward_one(0)
    own_sends(1)
    for q in range(4):
        gather(0, q)
    forward_two(0)
    gather(0, 4)
    finish(0)
    for q in (5, 6, 7):
        gather(0, q)
    merge_labels(0)

    forward_one(1)
    own_sends(2)
    reduce_one(0)
    for q in range(4):
        gather(1, q)
    forward_two(1)
    gather(1, 4)
    reduce_two(0)
    finish(1)
    refine(0)
    for q in (5, 6, 7):
        gather(1, q)
    merge_labels(1)

    forward_one(2)
    spread_one(0)
    reduce_one(1)
    for q in range(4):
        gather(2, q)
    forward_two(2)
    gather(2, 4)
    reduce_two(1)
    spread_two(0)
    finish(2)
    refine(1)
    for q in (5, 6, 7):
        gather(2, q)
    merge_labels(2)

    spread_one(1)
    settle(0)
    correlate(0, 0)
    reduce_one(2)
    correlate(0, 1)
    spread_two(1)
    correlate(0, 2)
    correlate(0, 3)
    reduce_two(2)
    settle(1)
    correlate(1, 0)
    refine(2)
    correlate(1, 1)
    spread_one(2)
    correlate(1, 2)
    correlate(1, 3)
    spread_two(2)
    settle(2)
    for d in range(4):
        correlate(2, d)
        collect(d)
    score_ref[...] = rows_ref[...].T[0:64]
    write_new()

    for c in tab_cp:
        c.wait_send()
    swaps[CHUNKS - 1].wait_send()
    for cc in range(CHUNKS):
        for c in hops[cc] + [halos[cc], x_sends[cc], x_gives[cc]]:
            c.wait_send()
        for c in y_sends[cc] + y_gives[cc] + passes[cc]:
            c.wait_send()


def refine_and_correlate(own, tab, old, scale):
    bf16, f32 = jnp.bfloat16, jnp.float32
    dma = pltpu.SemaphoreType.DMA
    vmem = pl.BlockSpec(memory_space=pltpu.VMEM)
    flat = FLAT * WIDE
    return pl.pallas_call(
        functools.partial(refine_kernel, scale),
        out_shape=(
            jax.ShapeDtypeStruct((64, 24 * TAPS), bf16),
            jax.ShapeDtypeStruct((64, 4096), f32),
        ),
        in_specs=[vmem, vmem, pl.BlockSpec(memory_space=pl.ANY)],
        out_specs=[vmem] * 2,
        scratch_shapes=[
            pltpu.VMEM((ROWS, CHUNKS * PHASES * WIDE), bf16),
            pltpu.VMEM((8, 2, 16, CHUNKS * STEP * WIDE), bf16),
            pltpu.VMEM((16, CHUNKS * LONG), bf16),
            pltpu.VMEM((LONG + 64, 16), f32),
            pltpu.VMEM((CHUNKS, 16, STEP * WIDE), f32),
            pltpu.VMEM((8, CAP, 128), jnp.int32),
            pltpu.VMEM((8, GROUPS * STEP * CAP, 1024), bf16),
            pltpu.VMEM((GROUPS, 64, STEP * WIDE), f32),
            pltpu.VMEM((4, 2, 2, 16, flat), f32),
            pltpu.VMEM((4, 2, 16, flat), f32),
            pltpu.VMEM((CHUNKS, 4, 2, 16, flat), f32),
            pltpu.VMEM((CHUNKS, 4, 2, 16, flat), bf16),
            pltpu.VMEM((CHUNKS, 3, 2, 16, flat), bf16),
            pltpu.VMEM((CHUNKS, 16, flat), f32),
            pltpu.VMEM((CHUNKS, 16, flat), bf16),
            pltpu.VMEM((CHUNKS, 16, flat), bf16),
            pltpu.VMEM((len(PLANES), ROWS, 256), f32),
            pltpu.VMEM((4096, 128), f32),
            pltpu.VMEM((1536, 128), f32),
            dma,
            dma((7,)),
            dma((7,)),
            dma((CHUNKS * 8,)),
            dma((CHUNKS * 8,)),
            dma((CHUNKS,)),
            dma((CHUNKS,)),
            dma((CHUNKS,)),
            dma((CHUNKS,)),
            dma((CHUNKS * 3,)),
            dma((CHUNKS * 3,)),
            dma((CHUNKS,)),
            dma((CHUNKS,)),
            dma((CHUNKS,)),
            dma((CHUNKS,)),
            dma((CHUNKS * 6,)),
            dma((CHUNKS * 6,)),
            dma((CHUNKS * 8,)),
            dma((CHUNKS * 8,)),
        ],
        compiler_params=pltpu.CompilerParams(
            collective_id=0, has_side_effects=True, vmem_limit_bytes=62 << 20
        ),
        name="refine_and_correlate",
    )(own, tab, old)


def body(recording, spike_times, unit_labels, old_templates):
    sub_rows = recording.shape[0]
    panel, feat = old_templates.shape
    spikes = spike_times.shape[0]
    t = lax.axis_index("tm")
    u = lax.axis_index("unit")
    start = spike_times - (t * 8 + u) * sub_rows - (TAPS - 1) // 2
    owner = unit_labels // panel
    within = unit_labels % panel
    before = jnp.arange(spikes)[None, :] < jnp.arange(spikes)[:, None]
    rank = jnp.sum(
        jnp.logical_and(owner[:, None] == owner[None, :], before).astype(jnp.int32), axis=1
    )
    slot = owner * CAP + rank
    hit = jnp.arange(8 * CAP)[:, None] == slot[None, :]
    start_of = jnp.sum(jnp.where(hit, start[None, :], 0), axis=1)
    label_of = jnp.sum(jnp.where(hit, within[None, :] + 1, 0), axis=1) - 1
    lane = jnp.arange(128)[None, :]
    tab = jnp.where(lane < 64, start_of[:, None], label_of[:, None]).reshape(8, CAP, 128)
    scale = 1.0 / (feat**0.5)
    return refine_and_correlate(recording, tab.astype(jnp.int32), old_templates, scale)


def solution(mesh):
    in_specs = (P(("tm", "unit"), None), P(("tm", "unit")), P(("tm", "unit")), P("unit", None))
    out_specs = (P("unit", "tm"), P("unit", "tm"))
    return jax.shard_map(body, mesh=mesh, in_specs=in_specs, out_specs=out_specs, check_vma=False)
```

```python
import functools

import jax
import jax.numpy as jnp
from jax import lax
from jax.experimental import pallas as pl
from jax.experimental.pallas import tpu as pltpu
from jax.sharding import PartitionSpec as P

MESH = pl.DeviceIdType.MESH
TAPS = 61
CAP = 8
GROUPS = 4
STEP = 16
PHASES = 8
LINES = 128
ROWS = 1056
TAIL = 16
CHUNKS = 3
WIDE = 128
FLAT = STEP + 1
SIZE = ROWS // 2
LONG = TAPS * WIDE


def dot_f32(a, b):
    return jnp.dot(a, b, preferred_element_type=jnp.float32)


def dot_nt(a, b):
    return lax.dot_general(a, b, (((1,), (1,)), ((), ())), preferred_element_type=jnp.float32)


PLANES = [(d, e) for d in range(4) for e in range(3 if d > 0 else 2)]


def refine_kernel(
    scale,
    own_ref,
    tab_ref,
    old_ref,
    new_ref,
    score_ref,
    x_ref,
    t_ref,
    old_rows,
    old_tall,
    old_wide,
    tabs,
    picks,
    snip,
    sums,
    away,
    swap_in,
    part,
    part_in,
    via_in,
    far_in,
    keep,
    side_out,
    side_in,
    y_ref,
    rows_ref,
    new_tall,
    old_s,
    tab_s,
    tab_r,
    ag_s,
    ag_r,
    halo_s,
    halo_r,
    swap_s,
    swap_r,
    ys_s,
    ys_r,
    xs_s,
    xs_r,
    xg_s,
    xg_r,
    yg_s,
    yg_r,
    fw_s,
    fw_r,
):
    t = lax.axis_index("tm")
    u = lax.axis_index("unit")
    core = lax.rem(t, 2)
    chip = t // 2
    yy = chip // 2
    xh = lax.rem(chip, 2)
    beside = yy * 2 + 1 - xh
    z = lax.rem(u, 4)
    side = u - z
    other = 4 - side
    zp = lax.rem(z + 1, 4)
    zm = lax.rem(z + 3, 4)
    zo = lax.rem(z + 2, 4)
    up, down, across = side + zp, side + zm, other + z

    ug = lax.rem(t, 4)
    tg = t // 4
    old_cp = pltpu.make_async_copy(
        old_ref.at[pl.ds(pl.multiple_of(ug * 16, 16), 16)], old_rows, old_s
    )
    old_cp.start()

    barrier = pltpu.get_barrier_semaphore()
    for rel in range(1, 8):
        pl.semaphore_signal(
            barrier, inc=1, device_id={"unit": lax.rem(u + rel, 8)}, device_id_type=MESH
        )
    for rel in range(1, 16):
        pl.semaphore_signal(
            barrier, inc=1, device_id={"tm": lax.rem(t + rel, 16)}, device_id_type=MESH
        )
    row = lax.broadcasted_iota(jnp.int32, (LINES, 1024), 0) * PHASES
    col = lax.broadcasted_iota(jnp.int32, (LINES, 1024), 1)
    mine = pl.ds(pl.multiple_of(u * LINES, LINES), LINES)

    def sort_phases(first, last):
        own = own_ref[:, first * WIDE : last * WIDE]
        for p in range(PHASES):
            pick = jnp.where(col == row + p, 1.0, 0.0).astype(jnp.bfloat16)
            got = dot_f32(pick, own).astype(jnp.bfloat16)
            for cc in range(first, last):
                lane = (cc * PHASES + p) * WIDE
                x_ref[mine, lane : lane + WIDE] = got[
                    :, (cc - first) * WIDE : (cc - first + 1) * WIDE
                ]

    def block(index, cc, first=0, count=LINES):
        return x_ref.at[
            pl.ds(pl.multiple_of(index * LINES + first, 16), count),
            cc * PHASES * WIDE : (cc + 1) * PHASES * WIDE,
        ]

    def remote(src, dst, send, recv, where):
        return pltpu.make_async_remote_copy(
            src_ref=src,
            dst_ref=dst,
            send_sem=send,
            recv_sem=recv,
            device_id=where,
            device_id_type=MESH,
        )

    def hop(cc, k, ref, to):
        return remote(ref, ref, ag_s.at[cc * 14 + k], ag_r.at[cc * 14 + k], {"unit": to})

    half = LINES // 2

    def plan(cc):
        def low(index):
            return block(index, cc, 0, half)

        def high(index):
            return block(index, cc, half, half)

        pairs = [
            (low(u), across),
            (high(u), across),
            (low(u), up),
            (high(u), up),
            (low(u), down),
            (high(u), down),
            (low(down), up),
            (high(up), down),
            (low(across), up),
            (low(across), down),
            (high(across), up),
            (high(across), down),
            (low(side + zo), across),
            (high(side + zo), across),
        ]
        return [hop(cc, k, ref, to) for k, (ref, to) in enumerate(pairs)]

    hops = [plan(cc) for cc in range(CHUNKS)]

    def own_sends(cc):
        for k in (2, 5, 0, 3, 4, 1):
            hops[cc][k].start()

    def arrive_then(cc, k, *forwards):
        hops[cc][k].wait_recv()
        for f in forwards:
            hops[cc][f].start()

    def forward_a(cc):
        arrive_then(cc, 2, 6)
        arrive_then(cc, 5, 7)
        arrive_then(cc, 0, 8, 9)

    def forward_b(cc):
        arrive_then(cc, 1, 10, 11)

    def forward_two(cc):
        arrive_then(cc, 6, 12)
        arrive_then(cc, 7, 13)

    def near(cc):
        arrive_then(cc, 3)
        arrive_then(cc, 4)

    def finish(cc):
        for k in (8, 9, 10, 11, 12, 13):
            arrive_then(cc, k)
        halos[cc].start()

    def halo(cc):
        lanes = pl.ds(cc * PHASES * WIDE, PHASES * WIDE)
        return remote(
            x_ref.at[pl.ds(0, TAIL), lanes],
            x_ref.at[pl.ds(1024, TAIL), lanes],
            halo_s.at[cc],
            halo_r.at[cc],
            {"tm": lax.rem(t + 15, 16)},
        )

    halos = [halo(cc) for cc in range(CHUNKS)]

    sort_phases(0, 1)
    pl.semaphore_wait(barrier, 22)
    own_sends(0)
    tab_cp = []
    for rel in range(1, 8):
        to = lax.rem(u + rel, 8)
        c = remote(
            tab_ref.at[to], tabs.at[u], tab_s.at[rel - 1], tab_r.at[rel - 1], {"unit": to}
        )
        c.start()
        tab_cp.append(c)
    sort_phases(1, CHUNKS)
    forward_a(0)
    tabs[u] = tab_ref[u]
    for c in tab_cp:
        c.wait_recv()

    tval = lax.broadcasted_iota(jnp.int32, (CAP, 1024), 1)
    tval = (tval % LINES) * PHASES + tval // LINES
    lead = lax.broadcasted_iota(jnp.int32, (GROUPS * STEP, 1, 1), 0)
    tap = (lead % GROUPS) * STEP + lead // GROUPS
    tap = jnp.where(tap < TAPS, tap, -100000)
    order = [u, across, up, down, side + zo, other + zp, other + zm, other + zo]

    def build_picks(i, carry):
        start = tabs[i][:, 0:1]
        gap = (tval - start)[None]
        pick = jnp.where(gap == tap, 1.0, 0.0).reshape(GROUPS * STEP * CAP, 1024)
        picks[i] = pick.astype(jnp.bfloat16)
        return carry

    lax.fori_loop(0, 8, build_picks, 0)

    labels = tabs[...].reshape(64, 128)[:, 64:65]
    labels = jnp.concatenate([labels] * GROUPS, axis=0)
    r4 = lax.broadcasted_iota(jnp.int32, (256, 256), 0)
    c4 = lax.broadcasted_iota(jnp.int32, (256, 256), 1)
    merge = jnp.where(
        jnp.logical_and(labels == c4 % 64, r4 // 64 == c4 // 64), 1.0, 0.0
    )
    merge = merge.T.astype(jnp.bfloat16)
    tally = dot_f32(merge, jnp.ones((256, WIDE), jnp.bfloat16))

    def relay_old():
        old_cp.wait()
        for cc in range(CHUNKS):

            def turn(i, carry):
                src = pl.ds(pl.multiple_of(cc * LONG + i * 128, 128), 128)
                at = pl.ds(pl.multiple_of(i * 128, 128), 128)
                old_tall[at, :] = old_rows[:, src].astype(jnp.float32).T
                return carry

            lax.fori_loop(0, TAPS, turn, 0, unroll=True)
            for j in range(STEP):
                piece = old_tall[pl.ds(tg * STEP + j, WIDE, stride=TAPS), :].T
                piece = jnp.where(tg * STEP + j < TAPS, piece, 0.0)
                old_wide[cc, :, j * WIDE : (j + 1) * WIDE] = piece

    def gather(cc, position):
        b = order[position]
        base = cc * PHASES * WIDE
        rows = pl.ds(pl.multiple_of(b * LINES, LINES), LINES)
        data = jnp.concatenate(
            [x_ref[rows, base + p * WIDE : base + (p + 1) * WIDE] for p in range(PHASES)],
            axis=0,
        )
        cut = dot_f32(picks[b], data)
        at = pl.ds(pl.multiple_of(b * CAP, CAP), CAP)
        for j in range(STEP):
            for g in range(GROUPS):
                r = (j * GROUPS + g) * CAP
                snip[g, at, j * WIDE : (j + 1) * WIDE] = cut[r : r + CAP]

    swaps = [
        remote(away, swap_in.at[cc], swap_s.at[cc], swap_r.at[cc], {"tm": chip * 2 + 1 - core})
        for cc in range(CHUNKS)
    ]

    def merge_labels(cc):
        if cc > 0:
            swaps[cc - 1].wait_send()
        out = dot_f32(merge, snip[...].reshape(256, STEP * WIDE).astype(jnp.bfloat16))
        out = jnp.concatenate([out, tally], axis=1).reshape(4, 2, 2, 16, FLAT * WIDE)
        sums[cc] = out
        away[...] = sums[cc, :, :, 1 - core]
        swaps[cc].start()

    y_up, y_down, y_far = lax.rem(yy + 1, 4), lax.rem(yy + 3, 4), lax.rem(yy + 2, 4)
    to_up = {"tm": (y_up * 2 + xh) * 2 + core}
    to_down = {"tm": (y_down * 2 + xh) * 2 + core}

    def y_plan(cc):
        pairs = [
            (part.at[cc, y_far, 0], via_in.at[cc, 0], to_up),
            (part.at[cc, y_far, 1], via_in.at[cc, 1], to_down),
            (part.at[cc, y_up], part_in.at[cc, 0], to_up),
            (part.at[cc, y_down], part_in.at[cc, 1], to_down),
            (via_in.at[cc, 0], far_in.at[cc, 0], to_up),
            (via_in.at[cc, 1], far_in.at[cc, 1], to_down),
        ]
        return [
            remote(src, dst, ys_s.at[cc * 6 + k], ys_r.at[cc * 6 + k], to)
            for k, (src, dst, to) in enumerate(pairs)
        ]

    y_sends = [y_plan(cc) for cc in range(CHUNKS)]
    x_sends = [
        remote(side_out.at[cc], side_in.at[cc], xs_s.at[cc], xs_r.at[cc], {"tm": beside * 2 + core})
        for cc in range(CHUNKS)
    ]

    def reduce_one(cc):
        swaps[cc].wait_recv()
        both = sums[cc, :, :, core] + swap_in[cc]
        part[cc] = both.astype(jnp.bfloat16)
        for c in y_sends[cc][:4]:
            c.start()
        sums[cc, :, :, core] = both

    def relay_sums(cc):
        for k in (0, 1):
            y_sends[cc][k].wait_recv()
            y_sends[cc][4 + k].start()

    def reduce_two(cc):
        for c in y_sends[cc][2:]:
            c.wait_recv()

        def total(x):
            value = sums[cc, yy, x, core] + far_in[cc, x].astype(jnp.float32)
            for k in (0, 1):
                value = value + part_in[cc, k, x].astype(jnp.float32)
            return value

        side_out[cc] = total(1 - xh).astype(jnp.bfloat16)
        x_sends[cc].start()
        keep[cc] = total(xh)

    def panel(cc, ch, co):
        return t_ref.at[ch, co, :, cc * STEP * WIDE : (cc + 1) * STEP * WIDE]

    def x_give(cc):
        ref = panel(cc, chip, core)
        return remote(ref, ref, xg_s.at[cc], xg_r.at[cc], {"tm": beside * 2 + core})

    def y_give_plan(cc):
        pairs = [
            (chip, to_up),
            (chip, to_down),
            (beside, to_up),
            (beside, to_down),
            (y_down * 2 + xh, to_up),
            (y_up * 2 + 1 - xh, to_down),
        ]
        out = []
        for k, (ch, to) in enumerate(pairs):
            ref = panel(cc, ch, core)
            out.append(remote(ref, ref, yg_s.at[cc * 6 + k], yg_r.at[cc * 6 + k], to))
        return out

    def pass_on(cc, k, ch):
        ref = panel(cc, ch, core)
        return remote(
            ref, ref, fw_s.at[cc * 8 + k], fw_r.at[cc * 8 + k], {"tm": chip * 2 + 1 - core}
        )

    x_gives = [x_give(cc) for cc in range(CHUNKS)]
    y_gives = [y_give_plan(cc) for cc in range(CHUNKS)]
    origin = [
        chip,
        beside,
        y_down * 2 + xh,
        y_up * 2 + xh,
        y_down * 2 + 1 - xh,
        y_up * 2 + 1 - xh,
        y_far * 2 + xh,
        y_far * 2 + 1 - xh,
    ]
    passes = [[pass_on(cc, k, origin[k]) for k in range(8)] for cc in range(CHUNKS)]

    def refine(cc):
        x_sends[cc].wait_recv()
        total = keep[cc] + side_in[cc].astype(jnp.float32)
        counts = total[:, STEP * WIDE :]
        weight = counts / (counts + 4.0)
        safe = jnp.maximum(counts, 1.0)
        fresh = []
        for j in range(STEP):
            lanes = slice(j * WIDE, (j + 1) * WIDE)
            base = old_wide[cc, :, lanes]
            fresh.append(base + weight * (total[:, lanes] / safe - base))
        t_ref[chip, core, :, cc * STEP * WIDE : (cc + 1) * STEP * WIDE] = jnp.concatenate(
            fresh, axis=1
        ).astype(jnp.bfloat16)
        x_gives[cc].start()
        for c in y_gives[cc][:2]:
            c.start()
        passes[cc][0].start()

    def spread_one(cc):
        x_gives[cc].wait_recv()
        for c in y_gives[cc][2:4]:
            c.start()
        passes[cc][1].start()

    def spread_two(cc):
        for k, then in ((0, 4), (3, 5), (1, None), (2, None)):
            y_gives[cc][k].wait_recv()
            if then is not None:
                y_gives[cc][then].start()
            passes[cc][2 + k].start()

    def spread_three(cc):
        for k in (4, 5):
            y_gives[cc][k].wait_recv()
            passes[cc][2 + k].start()

    def settle(cc):
        for c in passes[cc]:
            c.wait_recv()
        halos[cc].wait_recv()

        @pl.when(t == 15)
        def _():
            x_ref[1024 : 1024 + TAIL, cc * PHASES * WIDE : (cc + 1) * PHASES * WIDE] = jnp.zeros(
                (TAIL, PHASES * WIDE), jnp.bfloat16
            )

    def correlate(cc, d):
        def one(i, carry):
            first = pl.multiple_of(i * SIZE, 16)
            for at, (dd, e) in enumerate(PLANES):
                if dd != d:
                    continue
                low = max(0, 8 * e - 2 * d)
                high = min(STEP, 8 * e + 8 - 2 * d)
                xl = (cc * PHASES + 2 * d + low - 8 * e) * WIDE
                tl = (cc * STEP + low) * WIDE
                span = (high - low) * WIDE
                panels = t_ref[:, :, :, tl : tl + span].reshape(256, span)
                total = dot_nt(x_ref[pl.ds(first, SIZE), xl : xl + span], panels)
                if cc == 0:
                    y_ref[at, pl.ds(first, SIZE), :] = total
                else:
                    y_ref[at, pl.ds(first, SIZE), :] += total
            return carry

        lax.fori_loop(0, 2, one, 0)

    def collect(d):
        a = None
        for at, (dd, e) in enumerate(PLANES):
            if dd != d:
                continue
            b = y_ref[at, e : e + 1032, 0:128] + y_ref[at, e + 4 : e + 4 + 1032, 128:256]
            a = b if a is None else a + b
        f = a[0:1024, 0:64] + a[2 : 2 + 1024, 64:128]
        rows_ref[pl.ds(d, 1024, stride=4), 0:64] = f * scale

    def write_new():
        want = lax.broadcasted_iota(jnp.int32, (32, WIDE), 1) - t * 24
        place = lax.broadcasted_iota(jnp.int32, (32, WIDE), 0)
        chosen = [
            jnp.where(jnp.logical_and(want + cc * WIDE == place, place < 24), 1.0, 0.0).astype(
                jnp.bfloat16
            )
            for cc in range(CHUNKS)
        ]
        for j in range(STEP):
            acc = None
            for cc in range(CHUNKS):
                lane = (cc * STEP + j) * WIDE
                piece = t_ref[:, :, :, lane : lane + WIDE].reshape(256, WIDE)
                piece = dot_nt(chosen[cc], piece)
                acc = piece if acc is None else acc + piece
            for g in range(GROUPS):
                if g * STEP + j < TAPS:
                    new_tall[pl.ds(g * STEP + j, 24, stride=TAPS), 0:64] = acc[
                        0:24, g * 64 : (g + 1) * 64
                    ]
        new_ref[...] = new_tall[...].T[0:64, 0 : 24 * TAPS].astype(jnp.bfloat16)

    def gather_many(cc, positions):
        for q in positions:
            gather(cc, q)

    forward_b(0)
    own_sends(1)
    relay_old()
    forward_two(0)
    near(0)
    gather_many(0, (0, 1, 2, 3))
    forward_a(1)
    gather(0, 4)
    forward_b(1)
    own_sends(2)
    finish(0)
    gather_many(0, (5, 6, 7))
    merge_labels(0)

    forward_two(1)
    near(1)
    gather_many(1, (0, 1, 2))
    reduce_one(0)
    forward_a(2)
    gather_many(1, (3, 4))
    relay_sums(0)
    forward_b(2)
    finish(1)
    forward_two(2)
    gather_many(1, (5, 6, 7))
    merge_labels(1)
    reduce_two(0)

    near(2)
    gather_many(2, (0, 1, 2))
    reduce_one(1)
    refine(0)
    gather_many(2, (3, 4))
    relay_sums(1)
    spread_one(0)
    finish(2)
    gather_many(2, (5, 6, 7))
    merge_labels(2)

    spread_two(0)
    reduce_two(1)
    reduce_one(2)
    spread_three(0)
    refine(1)
    relay_sums(2)
    settle(0)
    correlate(0, 0)
    spread_one(1)
    correlate(0, 1)
    spread_two(1)
    reduce_two(2)
    correlate(0, 2)
    spread_three(1)
    correlate(0, 3)
    refine(2)
    settle(1)
    correlate(1, 0)
    correlate(1, 1)
    spread_one(2)
    correlate(1, 2)
    spread_two(2)
    correlate(1, 3)
    spread_three(2)
    settle(2)
    for d in range(4):
        correlate(2, d)
        collect(d)
    score_ref[...] = rows_ref[...].T[0:64]
    write_new()

    for c in tab_cp:
        c.wait_send()
    swaps[CHUNKS - 1].wait_send()
    for cc in range(CHUNKS):
        for c in hops[cc] + [halos[cc], x_sends[cc], x_gives[cc]]:
            c.wait_send()
        for c in y_sends[cc] + y_gives[cc] + passes[cc]:
            c.wait_send()


def refine_and_correlate(own, tab, old, scale):
    bf16, f32 = jnp.bfloat16, jnp.float32
    dma = pltpu.SemaphoreType.DMA
    vmem = pl.BlockSpec(memory_space=pltpu.VMEM)
    flat = FLAT * WIDE
    return pl.pallas_call(
        functools.partial(refine_kernel, scale),
        out_shape=(
            jax.ShapeDtypeStruct((64, 24 * TAPS), bf16),
            jax.ShapeDtypeStruct((64, 4096), f32),
        ),
        in_specs=[vmem, vmem, pl.BlockSpec(memory_space=pl.ANY)],
        out_specs=[vmem] * 2,
        scratch_shapes=[
            pltpu.VMEM((ROWS, CHUNKS * PHASES * WIDE), bf16),
            pltpu.VMEM((8, 2, 16, CHUNKS * STEP * WIDE), bf16),
            pltpu.VMEM((16, CHUNKS * LONG), bf16),
            pltpu.VMEM((LONG + 64, 16), f32),
            pltpu.VMEM((CHUNKS, 16, STEP * WIDE), f32),
            pltpu.VMEM((8, CAP, 128), jnp.int32),
            pltpu.VMEM((8, GROUPS * STEP * CAP, 1024), bf16),
            pltpu.VMEM((GROUPS, 64, STEP * WIDE), f32),
            pltpu.VMEM((CHUNKS, 4, 2, 2, 16, flat), f32),
            pltpu.VMEM((4, 2, 16, flat), f32),
            pltpu.VMEM((CHUNKS, 4, 2, 16, flat), f32),
            pltpu.VMEM((CHUNKS, 4, 2, 16, flat), bf16),
            pltpu.VMEM((CHUNKS, 2, 2, 16, flat), bf16),
            pltpu.VMEM((CHUNKS, 2, 16, flat), bf16),
            pltpu.VMEM((CHUNKS, 2, 16, flat), bf16),
            pltpu.VMEM((CHUNKS, 16, flat), f32),
            pltpu.VMEM((CHUNKS, 16, flat), bf16),
            pltpu.VMEM((CHUNKS, 16, flat), bf16),
            pltpu.VMEM((len(PLANES), ROWS, 256), f32),
            pltpu.VMEM((4096, 128), f32),
            pltpu.VMEM((1536, 128), f32),
            dma,
            dma((7,)),
            dma((7,)),
            dma((CHUNKS * 14,)),
            dma((CHUNKS * 14,)),
            dma((CHUNKS,)),
            dma((CHUNKS,)),
            dma((CHUNKS,)),
            dma((CHUNKS,)),
            dma((CHUNKS * 6,)),
            dma((CHUNKS * 6,)),
            dma((CHUNKS,)),
            dma((CHUNKS,)),
            dma((CHUNKS,)),
            dma((CHUNKS,)),
            dma((CHUNKS * 6,)),
            dma((CHUNKS * 6,)),
            dma((CHUNKS * 8,)),
            dma((CHUNKS * 8,)),
        ],
        compiler_params=pltpu.CompilerParams(
            collective_id=0, has_side_effects=True, vmem_limit_bytes=62 << 20
        ),
        name="refine_and_correlate",
    )(own, tab, old)


def body(recording, spike_times, unit_labels, old_templates):
    sub_rows = recording.shape[0]
    panel, feat = old_templates.shape
    spikes = spike_times.shape[0]
    t = lax.axis_index("tm")
    u = lax.axis_index("unit")
    start = spike_times - (t * 8 + u) * sub_rows - (TAPS - 1) // 2
    owner = unit_labels // panel
    within = unit_labels % panel
    before = jnp.arange(spikes)[None, :] < jnp.arange(spikes)[:, None]
    rank = jnp.sum(
        jnp.logical_and(owner[:, None] == owner[None, :], before).astype(jnp.int32), axis=1
    )
    slot = owner * CAP + rank
    hit = jnp.arange(8 * CAP)[:, None] == slot[None, :]
    start_of = jnp.sum(jnp.where(hit, start[None, :], 0), axis=1)
    label_of = jnp.sum(jnp.where(hit, within[None, :] + 1, 0), axis=1) - 1
    lane = jnp.arange(128)[None, :]
    tab = jnp.where(lane < 64, start_of[:, None], label_of[:, None]).reshape(8, CAP, 128)
    scale = 1.0 / (feat**0.5)
    return refine_and_correlate(recording, tab.astype(jnp.int32), old_templates, scale)


def solution(mesh):
    in_specs = (P(("tm", "unit"), None), P(("tm", "unit")), P(("tm", "unit")), P("unit", None))
    out_specs = (P("unit", "tm"), P("unit", "tm"))
    return jax.shard_map(body, mesh=mesh, in_specs=in_specs, out_specs=out_specs, check_vma=False)
```

```python
import functools

import jax
import jax.numpy as jnp
from jax import lax
from jax.experimental import pallas as pl
from jax.experimental.pallas import tpu as pltpu
from jax.sharding import PartitionSpec as P

MESH = pl.DeviceIdType.MESH
TAPS = 61
CAP = 8
GROUPS = 4
STEP = 16
PHASES = 8
LINES = 128
ROWS = 1056
TAIL = 16
CHUNKS = 3
WIDE = 128
FLAT = STEP + 1
SIZE = 1040
LONG = TAPS * WIDE


def dot_f32(a, b):
    return jnp.dot(a, b, preferred_element_type=jnp.float32)


def dot_nt(a, b):
    return lax.dot_general(a, b, (((1,), (1,)), ((), ())), preferred_element_type=jnp.float32)


PLANES = [(d, e) for d in range(4) for e in range(3 if d > 0 else 2)]


def refine_kernel(
    scale,
    own_ref,
    times_ref,
    labels_ref,
    old_ref,
    new_ref,
    score_ref,
    plain,
    tab_ref,
    x_ref,
    t_ref,
    old_rows,
    old_tall,
    old_wide,
    tabs,
    picks,
    snip,
    sums,
    away,
    swap_in,
    part,
    part_in,
    via_in,
    far_in,
    keep,
    side_out,
    side_in,
    y_ref,
    rows_ref,
    new_tall,
    old_s,
    tab_s,
    tab_r,
    ag_s,
    ag_r,
    halo_s,
    halo_r,
    swap_s,
    swap_r,
    ys_s,
    ys_r,
    xs_s,
    xs_r,
    xg_s,
    xg_r,
    yg_s,
    yg_r,
    fw_s,
    fw_r,
):
    t = lax.axis_index("tm")
    u = lax.axis_index("unit")
    core = lax.rem(t, 2)
    chip = t // 2
    yy = chip // 2
    xh = lax.rem(chip, 2)
    beside = yy * 2 + 1 - xh
    z = lax.rem(u, 4)
    side = u - z
    other = 4 - side
    zp = lax.rem(z + 1, 4)
    zm = lax.rem(z + 3, 4)
    zo = lax.rem(z + 2, 4)
    up, down, across = side + zp, side + zm, other + z

    ug = lax.rem(t, 4)
    tg = t // 4
    old_cp = pltpu.make_async_copy(
        old_ref.at[pl.ds(pl.multiple_of(ug * 16, 16), 16)], old_rows, old_s
    )
    old_cp.start()

    barrier = pltpu.get_barrier_semaphore()
    for rel in range(1, 8):
        pl.semaphore_signal(
            barrier, inc=1, device_id={"unit": lax.rem(u + rel, 8)}, device_id_type=MESH
        )
    for rel in range(1, 16):
        pl.semaphore_signal(
            barrier, inc=1, device_id={"tm": lax.rem(t + rel, 16)}, device_id_type=MESH
        )
    mine = pl.ds(pl.multiple_of(u * LINES, LINES), LINES)

    def sort_phases(cc):
        plain[...] = own_ref[:, cc * WIDE : (cc + 1) * WIDE].astype(jnp.float32)
        for p in range(PHASES):
            lane = (cc * PHASES + p) * WIDE
            got = plain[pl.ds(p, LINES, stride=PHASES), :]
            x_ref[mine, lane : lane + WIDE] = got.astype(jnp.bfloat16)

    def build_table():
        f32 = jnp.float32
        labels = labels_ref[...]
        start = (times_ref[...] - (t * 8 + u) * 1024 - (TAPS - 1) // 2).astype(f32)
        owner = lax.shift_right_logical(labels, 6).astype(f32)
        within = jnp.bitwise_and(labels, 63).astype(f32)
        spikes = labels.shape[1]
        i0 = lax.broadcasted_iota(jnp.int32, (spikes, spikes), 0)
        i1 = lax.broadcasted_iota(jnp.int32, (spikes, spikes), 1)
        owner_tall = jnp.sum(jnp.where(i0 == i1, owner, 0.0), axis=1, keepdims=True)
        ahead = jnp.logical_and(owner_tall == owner, i0 < i1)
        rank = jnp.sum(jnp.where(ahead, 1.0, 0.0), axis=0, keepdims=True)
        slot = owner * CAP + rank
        place = lax.broadcasted_iota(jnp.int32, (8 * CAP, spikes), 0).astype(f32)
        hit = place == slot
        start_of = jnp.sum(jnp.where(hit, start, 0.0), axis=1, keepdims=True)
        label_of = jnp.sum(jnp.where(hit, within + 1.0, 0.0), axis=1, keepdims=True) - 1.0
        lane = lax.broadcasted_iota(jnp.int32, (8 * CAP, 128), 1)
        tab_ref[...] = jnp.where(lane < 64, start_of, label_of).reshape(8, CAP, 128)

    def block(index, cc, first=0, count=LINES):
        return x_ref.at[
            pl.ds(pl.multiple_of(index * LINES + first, 16), count),
            cc * PHASES * WIDE : (cc + 1) * PHASES * WIDE,
        ]

    def remote(src, dst, send, recv, where):
        return pltpu.make_async_remote_copy(
            src_ref=src,
            dst_ref=dst,
            send_sem=send,
            recv_sem=recv,
            device_id=where,
            device_id_type=MESH,
        )

    def hop(cc, k, ref, to):
        return remote(ref, ref, ag_s.at[cc * 14 + k], ag_r.at[cc * 14 + k], {"unit": to})

    half = LINES // 2

    def plan(cc):
        def low(index):
            return block(index, cc, 0, half)

        def high(index):
            return block(index, cc, half, half)

        pairs = [
            (low(u), across),
            (high(u), across),
            (low(u), up),
            (high(u), up),
            (low(u), down),
            (high(u), down),
            (low(down), up),
            (high(up), down),
            (low(across), up),
            (low(across), down),
            (high(across), up),
            (high(across), down),
            (low(side + zo), across),
            (high(side + zo), across),
        ]
        return [hop(cc, k, ref, to) for k, (ref, to) in enumerate(pairs)]

    hops = [plan(cc) for cc in range(CHUNKS)]

    def own_sends(cc):
        for k in (2, 5, 0, 3, 4, 1):
            hops[cc][k].start()

    def arrive_then(cc, k, *forwards):
        hops[cc][k].wait_recv()
        for f in forwards:
            hops[cc][f].start()

    def forward_a(cc):
        arrive_then(cc, 2, 6)
        arrive_then(cc, 5, 7)
        arrive_then(cc, 0, 8, 9)

    def forward_b(cc):
        arrive_then(cc, 1, 10, 11)

    def forward_two(cc):
        arrive_then(cc, 6, 12)
        arrive_then(cc, 7, 13)

    def near(cc):
        arrive_then(cc, 3)
        arrive_then(cc, 4)

    def finish(cc):
        for k in (8, 9, 10, 11, 12, 13):
            arrive_then(cc, k)
        halos[cc].start()

    def halo(cc):
        lanes = pl.ds(cc * PHASES * WIDE, PHASES * WIDE)
        return remote(
            x_ref.at[pl.ds(0, TAIL), lanes],
            x_ref.at[pl.ds(1024, TAIL), lanes],
            halo_s.at[cc],
            halo_r.at[cc],
            {"tm": lax.rem(t + 15, 16)},
        )

    halos = [halo(cc) for cc in range(CHUNKS)]

    sort_phases(0)
    pl.semaphore_wait(barrier, 22)
    own_sends(0)
    build_table()
    tab_cp = []
    for rel in range(1, 8):
        to = lax.rem(u + rel, 8)
        c = remote(
            tab_ref.at[to], tabs.at[u], tab_s.at[rel - 1], tab_r.at[rel - 1], {"unit": to}
        )
        c.start()
        tab_cp.append(c)
    sort_phases(1)
    sort_phases(2)
    forward_a(0)
    tabs[u] = tab_ref[u]
    for c in tab_cp:
        c.wait_recv()

    tval = lax.broadcasted_iota(jnp.int32, (CAP, 1024), 1)
    tval = ((tval % LINES) * PHASES + tval // LINES).astype(jnp.float32)
    lead = lax.broadcasted_iota(jnp.int32, (GROUPS * STEP, 1, 1), 0)
    tap = (lead % GROUPS) * STEP + lead // GROUPS
    tap = jnp.where(tap < TAPS, tap, -100000).astype(jnp.float32)
    order = [u, across, up, down, side + zo, other + zp, other + zm, other + zo]

    def build_picks(i, carry):
        start = tabs[i][:, 0:1]
        gap = (tval - start)[None]
        pick = jnp.where(gap == tap, 1.0, 0.0).reshape(GROUPS * STEP * CAP, 1024)
        picks[i] = pick.astype(jnp.bfloat16)
        return carry

    lax.fori_loop(0, 8, build_picks, 0)

    labels = tabs[...].reshape(64, 128)[:, 64:65]
    labels = jnp.concatenate([labels] * GROUPS, axis=0)
    r4 = lax.broadcasted_iota(jnp.int32, (256, 256), 0)
    c4 = lax.broadcasted_iota(jnp.int32, (256, 256), 1)
    unit_of = (c4 % 64).astype(jnp.float32)
    merge = jnp.where(
        jnp.logical_and(labels == unit_of, r4 // 64 == c4 // 64), 1.0, 0.0
    )
    merge = merge.T.astype(jnp.bfloat16)
    tally = dot_f32(merge, jnp.ones((256, WIDE), jnp.bfloat16))

    def relay_old():
        old_cp.wait()
        for cc in range(CHUNKS):

            def turn(i, carry):
                src = pl.ds(pl.multiple_of(cc * LONG + i * 128, 128), 128)
                at = pl.ds(pl.multiple_of(i * 128, 128), 128)
                old_tall[at, :] = old_rows[:, src].astype(jnp.float32).T
                return carry

            lax.fori_loop(0, TAPS, turn, 0, unroll=True)
            for j in range(STEP):
                piece = old_tall[pl.ds(tg * STEP + j, WIDE, stride=TAPS), :].T
                piece = jnp.where(tg * STEP + j < TAPS, piece, 0.0)
                old_wide[cc, :, j * WIDE : (j + 1) * WIDE] = piece

    def gather(cc, position):
        b = order[position]
        base = cc * PHASES * WIDE
        rows = pl.ds(pl.multiple_of(b * LINES, LINES), LINES)
        data = jnp.concatenate(
            [x_ref[rows, base + p * WIDE : base + (p + 1) * WIDE] for p in range(PHASES)],
            axis=0,
        )
        cut = dot_f32(picks[b], data)
        at = pl.ds(pl.multiple_of(b * CAP, CAP), CAP)
        for j in range(STEP):
            for g in range(GROUPS):
                r = (j * GROUPS + g) * CAP
                snip[g, at, j * WIDE : (j + 1) * WIDE] = cut[r : r + CAP]

    swaps = [
        remote(away, swap_in.at[cc], swap_s.at[cc], swap_r.at[cc], {"tm": chip * 2 + 1 - core})
        for cc in range(CHUNKS)
    ]

    def merge_labels(cc):
        if cc > 0:
            swaps[cc - 1].wait_send()
        out = dot_f32(merge, snip[...].reshape(256, STEP * WIDE).astype(jnp.bfloat16))
        out = jnp.concatenate([out, tally], axis=1).reshape(4, 2, 2, 16, FLAT * WIDE)
        sums[cc] = out
        away[...] = sums[cc, :, :, 1 - core]
        swaps[cc].start()

    y_up, y_down, y_far = lax.rem(yy + 1, 4), lax.rem(yy + 3, 4), lax.rem(yy + 2, 4)
    to_up = {"tm": (y_up * 2 + xh) * 2 + core}
    to_down = {"tm": (y_down * 2 + xh) * 2 + core}

    def y_plan(cc):
        pairs = [
            (part.at[cc, y_far, 0], via_in.at[cc, 0], to_up),
            (part.at[cc, y_far, 1], via_in.at[cc, 1], to_down),
            (part.at[cc, y_up], part_in.at[cc, 0], to_up),
            (part.at[cc, y_down], part_in.at[cc, 1], to_down),
            (via_in.at[cc, 0], far_in.at[cc, 0], to_up),
            (via_in.at[cc, 1], far_in.at[cc, 1], to_down),
        ]
        return [
            remote(src, dst, ys_s.at[cc * 6 + k], ys_r.at[cc * 6 + k], to)
            for k, (src, dst, to) in enumerate(pairs)
        ]

    y_sends = [y_plan(cc) for cc in range(CHUNKS)]
    x_sends = [
        remote(side_out.at[cc], side_in.at[cc], xs_s.at[cc], xs_r.at[cc], {"tm": beside * 2 + core})
        for cc in range(CHUNKS)
    ]

    def reduce_one(cc):
        swaps[cc].wait_recv()
        both = sums[cc, :, :, core] + swap_in[cc]
        part[cc] = both.astype(jnp.bfloat16)
        for c in y_sends[cc][:4]:
            c.start()
        sums[cc, :, :, core] = both

    def relay_sums(cc):
        for k in (0, 1):
            y_sends[cc][k].wait_recv()
            y_sends[cc][4 + k].start()

    def reduce_two(cc):
        for c in y_sends[cc][2:]:
            c.wait_recv()

        def total(x):
            value = sums[cc, yy, x, core] + far_in[cc, x].astype(jnp.float32)
            for k in (0, 1):
                value = value + part_in[cc, k, x].astype(jnp.float32)
            return value

        side_out[cc] = total(1 - xh).astype(jnp.bfloat16)
        x_sends[cc].start()
        keep[cc] = total(xh)

    def panel(cc, ch, co):
        return t_ref.at[ch, co, :, cc * STEP * WIDE : (cc + 1) * STEP * WIDE]

    def x_give(cc):
        ref = panel(cc, chip, core)
        return remote(ref, ref, xg_s.at[cc], xg_r.at[cc], {"tm": beside * 2 + core})

    def y_give_plan(cc):
        pairs = [
            (chip, to_up),
            (chip, to_down),
            (beside, to_up),
            (beside, to_down),
            (y_down * 2 + xh, to_up),
            (y_up * 2 + 1 - xh, to_down),
        ]
        out = []
        for k, (ch, to) in enumerate(pairs):
            ref = panel(cc, ch, core)
            out.append(remote(ref, ref, yg_s.at[cc * 6 + k], yg_r.at[cc * 6 + k], to))
        return out

    def pass_on(cc, k, ch):
        ref = panel(cc, ch, core)
        return remote(
            ref, ref, fw_s.at[cc * 8 + k], fw_r.at[cc * 8 + k], {"tm": chip * 2 + 1 - core}
        )

    x_gives = [x_give(cc) for cc in range(CHUNKS)]
    y_gives = [y_give_plan(cc) for cc in range(CHUNKS)]
    origin = [
        chip,
        beside,
        y_down * 2 + xh,
        y_up * 2 + xh,
        y_down * 2 + 1 - xh,
        y_up * 2 + 1 - xh,
        y_far * 2 + xh,
        y_far * 2 + 1 - xh,
    ]
    passes = [[pass_on(cc, k, origin[k]) for k in range(8)] for cc in range(CHUNKS)]

    def refine(cc):
        x_sends[cc].wait_recv()
        total = keep[cc] + side_in[cc].astype(jnp.float32)
        counts = total[:, STEP * WIDE :]
        weight = counts / (counts + 4.0)
        safe = jnp.maximum(counts, 1.0)
        fresh = []
        for j in range(STEP):
            lanes = slice(j * WIDE, (j + 1) * WIDE)
            base = old_wide[cc, :, lanes]
            fresh.append(base + weight * (total[:, lanes] / safe - base))
        t_ref[chip, core, :, cc * STEP * WIDE : (cc + 1) * STEP * WIDE] = jnp.concatenate(
            fresh, axis=1
        ).astype(jnp.bfloat16)
        x_gives[cc].start()
        for c in y_gives[cc][:2]:
            c.start()
        passes[cc][0].start()

    def spread_one(cc):
        x_gives[cc].wait_recv()
        for c in y_gives[cc][2:4]:
            c.start()
        passes[cc][1].start()

    def spread_two(cc):
        for k, then in ((0, 4), (3, 5), (1, None), (2, None)):
            y_gives[cc][k].wait_recv()
            if then is not None:
                y_gives[cc][then].start()
            passes[cc][2 + k].start()

    def spread_three(cc):
        for k in (4, 5):
            y_gives[cc][k].wait_recv()
            passes[cc][2 + k].start()

    def settle(cc):
        for c in passes[cc]:
            c.wait_recv()
        halos[cc].wait_recv()

        @pl.when(t == 15)
        def _():
            x_ref[1024 : 1024 + TAIL, cc * PHASES * WIDE : (cc + 1) * PHASES * WIDE] = jnp.zeros(
                (TAIL, PHASES * WIDE), jnp.bfloat16
            )

    def correlate(cc, d):
        def one(i, carry):
            first = 0
            for at, (dd, e) in enumerate(PLANES):
                if dd != d:
                    continue
                low = max(0, 8 * e - 2 * d)
                high = min(STEP, 8 * e + 8 - 2 * d)
                xl = (cc * PHASES + 2 * d + low - 8 * e) * WIDE
                tl = (cc * STEP + low) * WIDE
                span = (high - low) * WIDE
                panels = t_ref[:, :, :, tl : tl + span].reshape(256, span)
                total = dot_nt(x_ref[pl.ds(first, SIZE), xl : xl + span], panels)
                if cc == 0:
                    y_ref[at, pl.ds(first, SIZE), :] = total
                else:
                    y_ref[at, pl.ds(first, SIZE), :] += total
            return carry

        one(0, 0)

    def collect(d):
        a = None
        for at, (dd, e) in enumerate(PLANES):
            if dd != d:
                continue
            b = y_ref[at, e : e + 1032, 0:128] + y_ref[at, e + 4 : e + 4 + 1032, 128:256]
            a = b if a is None else a + b
        f = a[0:1024, 0:64] + a[2 : 2 + 1024, 64:128]
        rows_ref[pl.ds(d, 1024, stride=4), 0:64] = f * scale

    def write_new():
        want = lax.broadcasted_iota(jnp.int32, (32, WIDE), 1) - t * 24
        place = lax.broadcasted_iota(jnp.int32, (32, WIDE), 0)
        chosen = [
            jnp.where(jnp.logical_and(want + cc * WIDE == place, place < 24), 1.0, 0.0).astype(
                jnp.bfloat16
            )
            for cc in range(CHUNKS)
        ]
        for j in range(STEP):
            acc = None
            for cc in range(CHUNKS):
                lane = (cc * STEP + j) * WIDE
                piece = t_ref[:, :, :, lane : lane + WIDE].reshape(256, WIDE)
                piece = dot_nt(chosen[cc], piece)
                acc = piece if acc is None else acc + piece
            for g in range(GROUPS):
                if g * STEP + j < TAPS:
                    new_tall[pl.ds(g * STEP + j, 24, stride=TAPS), 0:64] = acc[
                        0:24, g * 64 : (g + 1) * 64
                    ]
        new_ref[...] = new_tall[...].T[0:64, 0 : 24 * TAPS].astype(jnp.bfloat16)

    def gather_many(cc, positions):
        for q in positions:
            gather(cc, q)

    forward_b(0)
    own_sends(1)
    relay_old()
    forward_two(0)
    near(0)
    gather_many(0, (0, 1, 2, 3))
    forward_a(1)
    gather(0, 4)
    forward_b(1)
    own_sends(2)
    finish(0)
    gather_many(0, (5, 6, 7))
    merge_labels(0)

    forward_two(1)
    near(1)
    gather_many(1, (0, 1, 2))
    reduce_one(0)
    forward_a(2)
    gather_many(1, (3, 4))
    relay_sums(0)
    forward_b(2)
    finish(1)
    forward_two(2)
    gather_many(1, (5, 6, 7))
    merge_labels(1)
    reduce_two(0)

    near(2)
    gather_many(2, (0, 1, 2))
    reduce_one(1)
    refine(0)
    gather_many(2, (3, 4))
    relay_sums(1)
    spread_one(0)
    finish(2)
    gather_many(2, (5, 6, 7))
    merge_labels(2)

    spread_two(0)
    reduce_two(1)
    reduce_one(2)
    spread_three(0)
    relay_sums(2)
    refine(1)
    settle(0)
    correlate(0, 0)
    correlate(0, 1)
    spread_one(1)
    reduce_two(2)
    correlate(0, 2)
    spread_two(1)
    correlate(0, 3)
    refine(2)
    spread_three(1)
    settle(1)
    correlate(1, 0)
    spread_one(2)
    correlate(1, 1)
    correlate(1, 2)
    spread_two(2)
    correlate(1, 3)
    spread_three(2)
    settle(2)
    for d in range(4):
        correlate(2, d)
        collect(d)
    score_ref[...] = rows_ref[...].T[0:64]
    write_new()

    for c in tab_cp:
        c.wait_send()
    swaps[CHUNKS - 1].wait_send()
    for cc in range(CHUNKS):
        for c in hops[cc] + [halos[cc], x_sends[cc], x_gives[cc]]:
            c.wait_send()
        for c in y_sends[cc] + y_gives[cc] + passes[cc]:
            c.wait_send()


def refine_and_correlate(own, times, labels, old, scale):
    bf16, f32 = jnp.bfloat16, jnp.float32
    dma = pltpu.SemaphoreType.DMA
    vmem = pl.BlockSpec(memory_space=pltpu.VMEM)
    flat = FLAT * WIDE
    return pl.pallas_call(
        functools.partial(refine_kernel, scale),
        out_shape=(
            jax.ShapeDtypeStruct((64, 24 * TAPS), bf16),
            jax.ShapeDtypeStruct((64, 4096), f32),
        ),
        in_specs=[vmem, vmem, vmem, pl.BlockSpec(memory_space=pl.ANY)],
        out_specs=[vmem] * 2,
        scratch_shapes=[
            pltpu.VMEM((1024, WIDE), f32),
            pltpu.VMEM((8, CAP, 128), f32),
            pltpu.VMEM((ROWS, CHUNKS * PHASES * WIDE), bf16),
            pltpu.VMEM((8, 2, 16, CHUNKS * STEP * WIDE), bf16),
            pltpu.VMEM((16, CHUNKS * LONG), bf16),
            pltpu.VMEM((LONG + 64, 16), f32),
            pltpu.VMEM((CHUNKS, 16, STEP * WIDE), f32),
            pltpu.VMEM((8, CAP, 128), f32),
            pltpu.VMEM((8, GROUPS * STEP * CAP, 1024), bf16),
            pltpu.VMEM((GROUPS, 64, STEP * WIDE), f32),
            pltpu.VMEM((CHUNKS, 4, 2, 2, 16, flat), f32),
            pltpu.VMEM((4, 2, 16, flat), f32),
            pltpu.VMEM((CHUNKS, 4, 2, 16, flat), f32),
            pltpu.VMEM((CHUNKS, 4, 2, 16, flat), bf16),
            pltpu.VMEM((CHUNKS, 2, 2, 16, flat), bf16),
            pltpu.VMEM((CHUNKS, 2, 16, flat), bf16),
            pltpu.VMEM((CHUNKS, 2, 16, flat), bf16),
            pltpu.VMEM((CHUNKS, 16, flat), f32),
            pltpu.VMEM((CHUNKS, 16, flat), bf16),
            pltpu.VMEM((CHUNKS, 16, flat), bf16),
            pltpu.VMEM((len(PLANES), ROWS, 256), f32),
            pltpu.VMEM((4096, 128), f32),
            pltpu.VMEM((1536, 128), f32),
            dma,
            dma((7,)),
            dma((7,)),
            dma((CHUNKS * 14,)),
            dma((CHUNKS * 14,)),
            dma((CHUNKS,)),
            dma((CHUNKS,)),
            dma((CHUNKS,)),
            dma((CHUNKS,)),
            dma((CHUNKS * 6,)),
            dma((CHUNKS * 6,)),
            dma((CHUNKS,)),
            dma((CHUNKS,)),
            dma((CHUNKS,)),
            dma((CHUNKS,)),
            dma((CHUNKS * 6,)),
            dma((CHUNKS * 6,)),
            dma((CHUNKS * 8,)),
            dma((CHUNKS * 8,)),
        ],
        compiler_params=pltpu.CompilerParams(
            collective_id=0, has_side_effects=True, vmem_limit_bytes=62 << 20
        ),
        name="refine_and_correlate",
    )(own, times, labels, old)


def body(recording, spike_times, unit_labels, old_templates):
    feat = old_templates.shape[1]
    times = spike_times.reshape(1, -1)
    labels = unit_labels.reshape(1, -1)
    return refine_and_correlate(recording, times, labels, old_templates, 1.0 / (feat**0.5))


def solution(mesh):
    in_specs = (P(("tm", "unit"), None), P(("tm", "unit")), P(("tm", "unit")), P("unit", None))
    out_specs = (P("unit", "tm"), P("unit", "tm"))
    return jax.shard_map(body, mesh=mesh, in_specs=in_specs, out_specs=out_specs, check_vma=False)
```

```python
import functools

import jax
import jax.numpy as jnp
from jax import lax
from jax.experimental import pallas as pl
from jax.experimental.pallas import tpu as pltpu
from jax.sharding import PartitionSpec as P

MESH = pl.DeviceIdType.MESH
TAPS = 61
CAP = 8
GROUPS = 4
STEP = 16
PHASES = 8
LINES = 128
ROWS = 1056
TAIL = 16
CHUNKS = 3
WIDE = 128
FLAT = STEP + 1
SIZE = 1040
LONG = TAPS * WIDE


def dot_f32(a, b):
    return jnp.dot(a, b, preferred_element_type=jnp.float32)


def dot_nt(a, b):
    return lax.dot_general(a, b, (((1,), (1,)), ((), ())), preferred_element_type=jnp.float32)


PLANES = [(d, e) for d in range(4) for e in range(3 if d > 0 else 2)]


def refine_kernel(
    scale,
    own_ref,
    times_ref,
    labels_ref,
    old_ref,
    new_ref,
    score_ref,
    plain,
    tab_ref,
    x_ref,
    t_ref,
    old_rows,
    old_tall,
    old_wide,
    tabs,
    picks,
    snip,
    sums,
    away,
    swap_in,
    part,
    part_in,
    via_in,
    far_in,
    keep,
    side_out,
    side_in,
    y_ref,
    rows_ref,
    new_tall,
    old_s,
    tab_s,
    tab_r,
    ag_s,
    ag_r,
    halo_s,
    halo_r,
    swap_s,
    swap_r,
    ys_s,
    ys_r,
    xs_s,
    xs_r,
    xg_s,
    xg_r,
    yg_s,
    yg_r,
    fw_s,
    fw_r,
):
    t = lax.axis_index("tm")
    u = lax.axis_index("unit")
    core = lax.rem(t, 2)
    chip = t // 2
    yy = chip // 2
    xh = lax.rem(chip, 2)
    beside = yy * 2 + 1 - xh
    z = lax.rem(u, 4)
    side = u - z
    other = 4 - side
    zp = lax.rem(z + 1, 4)
    zm = lax.rem(z + 3, 4)
    zo = lax.rem(z + 2, 4)
    up, down, across = side + zp, side + zm, other + z

    ug = lax.rem(t, 4)
    tg = t // 4
    old_cp = pltpu.make_async_copy(
        old_ref.at[pl.ds(pl.multiple_of(ug * 16, 16), 16)], old_rows, old_s
    )
    old_cp.start()

    barrier = pltpu.get_barrier_semaphore()
    for rel in range(1, 8):
        pl.semaphore_signal(
            barrier, inc=1, device_id={"unit": lax.rem(u + rel, 8)}, device_id_type=MESH
        )
    for rel in range(1, 16):
        pl.semaphore_signal(
            barrier, inc=1, device_id={"tm": lax.rem(t + rel, 16)}, device_id_type=MESH
        )
    mine = pl.ds(pl.multiple_of(u * LINES, LINES), LINES)

    def sort_phases(cc):
        plain[...] = own_ref[:, cc * WIDE : (cc + 1) * WIDE].astype(jnp.float32)
        for p in range(PHASES):
            lane = (cc * PHASES + p) * WIDE
            got = plain[pl.ds(p, LINES, stride=PHASES), :]
            x_ref[mine, lane : lane + WIDE] = got.astype(jnp.bfloat16)

    def build_table():
        f32 = jnp.float32
        labels = labels_ref[...]
        start = (times_ref[...] - (t * 8 + u) * 1024 - (TAPS - 1) // 2).astype(f32)
        owner = lax.shift_right_logical(labels, 6).astype(f32)
        within = jnp.bitwise_and(labels, 63).astype(f32)
        spikes = labels.shape[1]
        i0 = lax.broadcasted_iota(jnp.int32, (spikes, spikes), 0)
        i1 = lax.broadcasted_iota(jnp.int32, (spikes, spikes), 1)
        owner_tall = jnp.sum(jnp.where(i0 == i1, owner, 0.0), axis=1, keepdims=True)
        ahead = jnp.logical_and(owner_tall == owner, i0 < i1)
        rank = jnp.sum(jnp.where(ahead, 1.0, 0.0), axis=0, keepdims=True)
        slot = owner * CAP + rank
        place = lax.broadcasted_iota(jnp.int32, (8 * CAP, spikes), 0).astype(f32)
        hit = place == slot
        start_of = jnp.sum(jnp.where(hit, start, 0.0), axis=1, keepdims=True)
        label_of = jnp.sum(jnp.where(hit, within + 1.0, 0.0), axis=1, keepdims=True) - 1.0
        lane = lax.broadcasted_iota(jnp.int32, (8 * CAP, 128), 1)
        tab_ref[...] = jnp.where(lane < 64, start_of, label_of).reshape(8, CAP, 128)

    def block(index, cc, first=0, count=LINES):
        return x_ref.at[
            pl.ds(pl.multiple_of(index * LINES + first, 16), count),
            cc * PHASES * WIDE : (cc + 1) * PHASES * WIDE,
        ]

    def remote(src, dst, send, recv, where):
        return pltpu.make_async_remote_copy(
            src_ref=src,
            dst_ref=dst,
            send_sem=send,
            recv_sem=recv,
            device_id=where,
            device_id_type=MESH,
        )

    def hop(cc, k, ref, to):
        return remote(ref, ref, ag_s.at[cc * 14 + k], ag_r.at[cc * 14 + k], {"unit": to})

    half = LINES // 2

    def plan(cc):
        def low(index):
            return block(index, cc, 0, half)

        def high(index):
            return block(index, cc, half, half)

        pairs = [
            (low(u), across),
            (high(u), across),
            (low(u), up),
            (high(u), up),
            (low(u), down),
            (high(u), down),
            (low(down), up),
            (high(up), down),
            (low(across), up),
            (low(across), down),
            (high(across), up),
            (high(across), down),
            (low(side + zo), across),
            (high(side + zo), across),
        ]
        return [hop(cc, k, ref, to) for k, (ref, to) in enumerate(pairs)]

    hops = [plan(cc) for cc in range(CHUNKS)]

    def own_sends(cc):
        for k in (2, 5, 0, 3, 4, 1):
            hops[cc][k].start()

    def arrive_then(cc, k, *forwards):
        hops[cc][k].wait_recv()
        for f in forwards:
            hops[cc][f].start()

    def forward_a(cc):
        arrive_then(cc, 2, 6)
        arrive_then(cc, 5, 7)
        arrive_then(cc, 0, 8, 9)

    def forward_b(cc):
        arrive_then(cc, 1, 10, 11)

    def forward_two(cc):
        arrive_then(cc, 6, 12)
        arrive_then(cc, 7, 13)

    def near(cc):
        arrive_then(cc, 3)
        arrive_then(cc, 4)

    def finish(cc):
        for k in (8, 9, 10, 11, 12, 13):
            arrive_then(cc, k)
        halos[cc].start()

    def halo(cc):
        lanes = pl.ds(cc * PHASES * WIDE, PHASES * WIDE)
        return remote(
            x_ref.at[pl.ds(0, TAIL), lanes],
            x_ref.at[pl.ds(1024, TAIL), lanes],
            halo_s.at[cc],
            halo_r.at[cc],
            {"tm": lax.rem(t + 15, 16)},
        )

    halos = [halo(cc) for cc in range(CHUNKS)]

    sort_phases(0)
    pl.semaphore_wait(barrier, 22)
    own_sends(0)
    build_table()
    tab_cp = []
    for rel in range(1, 8):
        to = lax.rem(u + rel, 8)
        c = remote(
            tab_ref.at[to], tabs.at[u], tab_s.at[rel - 1], tab_r.at[rel - 1], {"unit": to}
        )
        c.start()
        tab_cp.append(c)
    sort_phases(1)
    sort_phases(2)
    forward_a(0)
    own_sends(1)
    tabs[u] = tab_ref[u]
    for c in tab_cp:
        c.wait_recv()

    tval = lax.broadcasted_iota(jnp.int32, (CAP, 1024), 1)
    tval = ((tval % LINES) * PHASES + tval // LINES).astype(jnp.float32)
    lead = lax.broadcasted_iota(jnp.int32, (GROUPS * STEP, 1, 1), 0)
    tap = (lead % GROUPS) * STEP + lead // GROUPS
    tap = jnp.where(tap < TAPS, tap, -100000).astype(jnp.float32)
    order = [u, across, up, down, side + zo, other + zp, other + zm, other + zo]

    def build_picks(i, carry):
        start = tabs[i][:, 0:1]
        gap = (tval - start)[None]
        pick = jnp.where(gap == tap, 1.0, 0.0).reshape(GROUPS * STEP * CAP, 1024)
        picks[i] = pick.astype(jnp.bfloat16)
        return carry

    lax.fori_loop(0, 8, build_picks, 0)

    labels = tabs[...].reshape(64, 128)[:, 64:65]
    labels = jnp.concatenate([labels] * GROUPS, axis=0)
    r4 = lax.broadcasted_iota(jnp.int32, (256, 256), 0)
    c4 = lax.broadcasted_iota(jnp.int32, (256, 256), 1)
    unit_of = (c4 % 64).astype(jnp.float32)
    merge = jnp.where(
        jnp.logical_and(labels == unit_of, r4 // 64 == c4 // 64), 1.0, 0.0
    )
    merge = merge.T.astype(jnp.bfloat16)
    tally = dot_f32(merge, jnp.ones((256, WIDE), jnp.bfloat16))

    def relay_old():
        old_cp.wait()
        for cc in range(CHUNKS):

            def turn(i, carry):
                src = pl.ds(pl.multiple_of(cc * LONG + i * 128, 128), 128)
                at = pl.ds(pl.multiple_of(i * 128, 128), 128)
                old_tall[at, :] = old_rows[:, src].astype(jnp.float32).T
                return carry

            lax.fori_loop(0, TAPS, turn, 0, unroll=True)
            for j in range(STEP):
                piece = old_tall[pl.ds(tg * STEP + j, WIDE, stride=TAPS), :].T
                piece = jnp.where(tg * STEP + j < TAPS, piece, 0.0)
                old_wide[cc, :, j * WIDE : (j + 1) * WIDE] = piece

    def gather(cc, position):
        b = order[position]
        base = cc * PHASES * WIDE
        rows = pl.ds(pl.multiple_of(b * LINES, LINES), LINES)
        data = jnp.concatenate(
            [x_ref[rows, base + p * WIDE : base + (p + 1) * WIDE] for p in range(PHASES)],
            axis=0,
        )
        cut = dot_f32(picks[b], data)
        at = pl.ds(pl.multiple_of(b * CAP, CAP), CAP)
        for j in range(STEP):
            for g in range(GROUPS):
                r = (j * GROUPS + g) * CAP
                snip[g, at, j * WIDE : (j + 1) * WIDE] = cut[r : r + CAP]

    swaps = [
        remote(away, swap_in.at[cc], swap_s.at[cc], swap_r.at[cc], {"tm": chip * 2 + 1 - core})
        for cc in range(CHUNKS)
    ]

    def merge_labels(cc):
        if cc > 0:
            swaps[cc - 1].wait_send()
        out = dot_f32(merge, snip[...].reshape(256, STEP * WIDE).astype(jnp.bfloat16))
        out = jnp.concatenate([out, tally], axis=1).reshape(4, 2, 2, 16, FLAT * WIDE)
        sums[cc] = out
        away[...] = sums[cc, :, :, 1 - core]
        swaps[cc].start()

    y_up, y_down, y_far = lax.rem(yy + 1, 4), lax.rem(yy + 3, 4), lax.rem(yy + 2, 4)
    to_up = {"tm": (y_up * 2 + xh) * 2 + core}
    to_down = {"tm": (y_down * 2 + xh) * 2 + core}

    def y_plan(cc):
        pairs = [
            (part.at[cc, y_far, 0], via_in.at[cc, 0], to_up),
            (part.at[cc, y_far, 1], via_in.at[cc, 1], to_down),
            (part.at[cc, y_up], part_in.at[cc, 0], to_up),
            (part.at[cc, y_down], part_in.at[cc, 1], to_down),
            (via_in.at[cc, 0], far_in.at[cc, 0], to_up),
            (via_in.at[cc, 1], far_in.at[cc, 1], to_down),
        ]
        return [
            remote(src, dst, ys_s.at[cc * 6 + k], ys_r.at[cc * 6 + k], to)
            for k, (src, dst, to) in enumerate(pairs)
        ]

    y_sends = [y_plan(cc) for cc in range(CHUNKS)]
    x_sends = [
        remote(side_out.at[cc], side_in.at[cc], xs_s.at[cc], xs_r.at[cc], {"tm": beside * 2 + core})
        for cc in range(CHUNKS)
    ]

    def reduce_one(cc):
        swaps[cc].wait_recv()
        both = sums[cc, :, :, core] + swap_in[cc]
        part[cc] = both.astype(jnp.bfloat16)
        for c in y_sends[cc][:4]:
            c.start()
        sums[cc, :, :, core] = both

    def relay_sums(cc):
        for k in (0, 1):
            y_sends[cc][k].wait_recv()
            y_sends[cc][4 + k].start()

    def reduce_two(cc):
        for c in y_sends[cc][2:]:
            c.wait_recv()

        def total(x):
            value = sums[cc, yy, x, core] + far_in[cc, x].astype(jnp.float32)
            for k in (0, 1):
                value = value + part_in[cc, k, x].astype(jnp.float32)
            return value

        side_out[cc] = total(1 - xh).astype(jnp.bfloat16)
        x_sends[cc].start()
        keep[cc] = total(xh)

    def panel(cc, ch, co):
        return t_ref.at[ch, co, :, cc * STEP * WIDE : (cc + 1) * STEP * WIDE]

    def x_give(cc):
        ref = panel(cc, chip, core)
        return remote(ref, ref, xg_s.at[cc], xg_r.at[cc], {"tm": beside * 2 + core})

    def y_give_plan(cc):
        pairs = [
            (chip, to_up),
            (chip, to_down),
            (beside, to_up),
            (beside, to_down),
            (y_down * 2 + xh, to_up),
            (y_up * 2 + 1 - xh, to_down),
        ]
        out = []
        for k, (ch, to) in enumerate(pairs):
            ref = panel(cc, ch, core)
            out.append(remote(ref, ref, yg_s.at[cc * 6 + k], yg_r.at[cc * 6 + k], to))
        return out

    def pass_on(cc, k, ch):
        ref = panel(cc, ch, core)
        return remote(
            ref, ref, fw_s.at[cc * 8 + k], fw_r.at[cc * 8 + k], {"tm": chip * 2 + 1 - core}
        )

    x_gives = [x_give(cc) for cc in range(CHUNKS)]
    y_gives = [y_give_plan(cc) for cc in range(CHUNKS)]
    origin = [
        chip,
        beside,
        y_down * 2 + xh,
        y_up * 2 + xh,
        y_down * 2 + 1 - xh,
        y_up * 2 + 1 - xh,
        y_far * 2 + xh,
        y_far * 2 + 1 - xh,
    ]
    passes = [[pass_on(cc, k, origin[k]) for k in range(8)] for cc in range(CHUNKS)]

    def refine(cc):
        x_sends[cc].wait_recv()
        total = keep[cc] + side_in[cc].astype(jnp.float32)
        counts = total[:, STEP * WIDE :]
        weight = counts / (counts + 4.0)
        safe = jnp.maximum(counts, 1.0)
        fresh = []
        for j in range(STEP):
            lanes = slice(j * WIDE, (j + 1) * WIDE)
            base = old_wide[cc, :, lanes]
            fresh.append(base + weight * (total[:, lanes] / safe - base))
        t_ref[chip, core, :, cc * STEP * WIDE : (cc + 1) * STEP * WIDE] = jnp.concatenate(
            fresh, axis=1
        ).astype(jnp.bfloat16)
        x_gives[cc].start()
        for c in y_gives[cc][:2]:
            c.start()
        passes[cc][0].start()

    def spread_one(cc):
        x_gives[cc].wait_recv()
        for c in y_gives[cc][2:4]:
            c.start()
        passes[cc][1].start()

    def spread_two(cc):
        for k, then in ((0, 4), (3, 5), (1, None), (2, None)):
            y_gives[cc][k].wait_recv()
            if then is not None:
                y_gives[cc][then].start()
            passes[cc][2 + k].start()

    def spread_three(cc):
        for k in (4, 5):
            y_gives[cc][k].wait_recv()
            passes[cc][2 + k].start()

    def settle(cc):
        for c in passes[cc]:
            c.wait_recv()
        halos[cc].wait_recv()

        @pl.when(t == 15)
        def _():
            x_ref[1024 : 1024 + TAIL, cc * PHASES * WIDE : (cc + 1) * PHASES * WIDE] = jnp.zeros(
                (TAIL, PHASES * WIDE), jnp.bfloat16
            )

    def correlate(cc, d):
        def one(i, carry):
            first = 0
            for at, (dd, e) in enumerate(PLANES):
                if dd != d:
                    continue
                low = max(0, 8 * e - 2 * d)
                high = min(STEP, 8 * e + 8 - 2 * d)
                xl = (cc * PHASES + 2 * d + low - 8 * e) * WIDE
                tl = (cc * STEP + low) * WIDE
                span = (high - low) * WIDE
                panels = t_ref[:, :, :, tl : tl + span].reshape(256, span)
                total = dot_nt(x_ref[pl.ds(first, SIZE), xl : xl + span], panels)
                if cc == 0:
                    y_ref[at, pl.ds(first, SIZE), :] = total
                else:
                    y_ref[at, pl.ds(first, SIZE), :] += total
            return carry

        one(0, 0)

    def collect(d):
        a = None
        for at, (dd, e) in enumerate(PLANES):
            if dd != d:
                continue
            b = y_ref[at, e : e + 1032, 0:128] + y_ref[at, e + 4 : e + 4 + 1032, 128:256]
            a = b if a is None else a + b
        f = a[0:1024, 0:64] + a[2 : 2 + 1024, 64:128]
        rows_ref[pl.ds(d, 1024, stride=4), 0:64] = f * scale

    def write_new():
        want = lax.broadcasted_iota(jnp.int32, (32, WIDE), 1) - t * 24
        place = lax.broadcasted_iota(jnp.int32, (32, WIDE), 0)
        chosen = [
            jnp.where(jnp.logical_and(want + cc * WIDE == place, place < 24), 1.0, 0.0).astype(
                jnp.bfloat16
            )
            for cc in range(CHUNKS)
        ]
        for j in range(STEP):
            acc = None
            for cc in range(CHUNKS):
                lane = (cc * STEP + j) * WIDE
                piece = t_ref[:, :, :, lane : lane + WIDE].reshape(256, WIDE)
                piece = dot_nt(chosen[cc], piece)
                acc = piece if acc is None else acc + piece
            for g in range(GROUPS):
                if g * STEP + j < TAPS:
                    new_tall[pl.ds(g * STEP + j, 24, stride=TAPS), 0:64] = acc[
                        0:24, g * 64 : (g + 1) * 64
                    ]
        new_ref[...] = new_tall[...].T[0:64, 0 : 24 * TAPS].astype(jnp.bfloat16)

    def gather_many(cc, positions):
        for q in positions:
            gather(cc, q)

    forward_b(0)
    relay_old()
    forward_two(0)
    near(0)
    gather_many(0, (0, 1, 2, 3))
    forward_a(1)
    own_sends(2)
    gather(0, 4)
    forward_b(1)
    finish(0)
    gather_many(0, (5, 6, 7))
    merge_labels(0)

    forward_two(1)
    near(1)
    gather_many(1, (0, 1, 2))
    reduce_one(0)
    forward_a(2)
    gather_many(1, (3, 4))
    relay_sums(0)
    forward_b(2)
    finish(1)
    forward_two(2)
    gather_many(1, (5, 6, 7))
    merge_labels(1)
    reduce_two(0)

    near(2)
    gather_many(2, (0, 1, 2))
    reduce_one(1)
    refine(0)
    gather_many(2, (3, 4))
    relay_sums(1)
    spread_one(0)
    finish(2)
    gather_many(2, (5, 6, 7))
    merge_labels(2)

    spread_two(0)
    reduce_two(1)
    reduce_one(2)
    spread_three(0)
    relay_sums(2)
    refine(1)
    settle(0)
    correlate(0, 0)
    correlate(0, 1)
    spread_one(1)
    reduce_two(2)
    correlate(0, 2)
    spread_two(1)
    correlate(0, 3)
    refine(2)
    spread_three(1)
    settle(1)
    correlate(1, 0)
    spread_one(2)
    correlate(1, 1)
    correlate(1, 2)
    spread_two(2)
    correlate(1, 3)
    spread_three(2)
    settle(2)
    for d in range(4):
        correlate(2, d)
        collect(d)
    score_ref[...] = rows_ref[...].T[0:64]
    write_new()

    for c in tab_cp:
        c.wait_send()
    swaps[CHUNKS - 1].wait_send()
    for cc in range(CHUNKS):
        for c in hops[cc] + [halos[cc], x_sends[cc], x_gives[cc]]:
            c.wait_send()
        for c in y_sends[cc] + y_gives[cc] + passes[cc]:
            c.wait_send()


def refine_and_correlate(own, times, labels, old, scale):
    bf16, f32 = jnp.bfloat16, jnp.float32
    dma = pltpu.SemaphoreType.DMA
    vmem = pl.BlockSpec(memory_space=pltpu.VMEM)
    flat = FLAT * WIDE
    return pl.pallas_call(
        functools.partial(refine_kernel, scale),
        out_shape=(
            jax.ShapeDtypeStruct((64, 24 * TAPS), bf16),
            jax.ShapeDtypeStruct((64, 4096), f32),
        ),
        in_specs=[vmem, vmem, vmem, pl.BlockSpec(memory_space=pl.ANY)],
        out_specs=[vmem] * 2,
        scratch_shapes=[
            pltpu.VMEM((1024, WIDE), f32),
            pltpu.VMEM((8, CAP, 128), f32),
            pltpu.VMEM((ROWS, CHUNKS * PHASES * WIDE), bf16),
            pltpu.VMEM((8, 2, 16, CHUNKS * STEP * WIDE), bf16),
            pltpu.VMEM((16, CHUNKS * LONG), bf16),
            pltpu.VMEM((LONG + 64, 16), f32),
            pltpu.VMEM((CHUNKS, 16, STEP * WIDE), f32),
            pltpu.VMEM((8, CAP, 128), f32),
            pltpu.VMEM((8, GROUPS * STEP * CAP, 1024), bf16),
            pltpu.VMEM((GROUPS, 64, STEP * WIDE), f32),
            pltpu.VMEM((CHUNKS, 4, 2, 2, 16, flat), f32),
            pltpu.VMEM((4, 2, 16, flat), f32),
            pltpu.VMEM((CHUNKS, 4, 2, 16, flat), f32),
            pltpu.VMEM((CHUNKS, 4, 2, 16, flat), bf16),
            pltpu.VMEM((CHUNKS, 2, 2, 16, flat), bf16),
            pltpu.VMEM((CHUNKS, 2, 16, flat), bf16),
            pltpu.VMEM((CHUNKS, 2, 16, flat), bf16),
            pltpu.VMEM((CHUNKS, 16, flat), f32),
            pltpu.VMEM((CHUNKS, 16, flat), bf16),
            pltpu.VMEM((CHUNKS, 16, flat), bf16),
            pltpu.VMEM((len(PLANES), ROWS, 256), f32),
            pltpu.VMEM((4096, 128), f32),
            pltpu.VMEM((1536, 128), f32),
            dma,
            dma((7,)),
            dma((7,)),
            dma((CHUNKS * 14,)),
            dma((CHUNKS * 14,)),
            dma((CHUNKS,)),
            dma((CHUNKS,)),
            dma((CHUNKS,)),
            dma((CHUNKS,)),
            dma((CHUNKS * 6,)),
            dma((CHUNKS * 6,)),
            dma((CHUNKS,)),
            dma((CHUNKS,)),
            dma((CHUNKS,)),
            dma((CHUNKS,)),
            dma((CHUNKS * 6,)),
            dma((CHUNKS * 6,)),
            dma((CHUNKS * 8,)),
            dma((CHUNKS * 8,)),
        ],
        compiler_params=pltpu.CompilerParams(
            collective_id=0, has_side_effects=True, vmem_limit_bytes=62 << 20
        ),
        name="refine_and_correlate",
    )(own, times, labels, old)


def body(recording, spike_times, unit_labels, old_templates):
    feat = old_templates.shape[1]
    times = spike_times.reshape(1, -1)
    labels = unit_labels.reshape(1, -1)
    return refine_and_correlate(recording, times, labels, old_templates, 1.0 / (feat**0.5))


def solution(mesh):
    in_specs = (P(("tm", "unit"), None), P(("tm", "unit")), P(("tm", "unit")), P("unit", None))
    out_specs = (P("unit", "tm"), P("unit", "tm"))
    return jax.shard_map(body, mesh=mesh, in_specs=in_specs, out_specs=out_specs, check_vma=False)
```
